128 devices in a mesh: shard: 32 (over x, z, core), tensor: 4 (over y).
Axes of the slice: x: 4, y: 4, z: 4, core: 2. Of those that a mesh axis runs over, the one named last changes fastest.
Arguments:
- gradients: bfloat16 [32, 1152, 1152], P(None, 'shard', 'tensor')
- weights: float32 [32, 1152, 1152], P(None, 'shard', 'tensor'), may hold values from -0.1875 to 0.1875
- owner_list: int32 [32], replicated, may hold values from 0 to 31, as said below
- left_gram_stats: float32 [64, 1152, 1152], P('shard', 'tensor'), may hold values from -6 to 6
- right_gram_stats: float32 [64, 1152, 1152], P('shard', 'tensor'), may hold values from -6 to 6
- left_root: bfloat16 [64, 1152, 1152], P('shard', None, 'tensor'), as said below
- right_root: bfloat16 [64, 1152, 1152], P('shard', None, 'tensor'), as said below
- adam_second_moment: float32 [64, 1152, 1152], P('shard', None, 'tensor'), may hold values from 0.1 to 10
Outputs:
- new_weights: float32 [32, 1152, 1152], P(None, 'shard', 'tensor')
- new_left: float32 [64, 1152, 1152], P('shard', 'tensor')
- new_right: float32 [64, 1152, 1152], P('shard', 'tensor')
- new_moment: float32 [64, 1152, 1152], P('shard', None, 'tensor')
The draws below stay inside these ranges and needn't reach their ends.
Inputs may be any that keep to these rules, and one draw needn't show every extreme that they name: `owner_list`: each owner index is named by at most 2 blocks, and some index by exactly 2. `left_root`: each slot's matrix is symmetric. `right_root`: each slot's matrix is symmetric.
All inputs are finite; a program needn't handle non-finite values.
Results may differ from the reference program's by a relative error of at most 0.0022.
Values may be sent and summed in bfloat16 or wider, within the bound.
No kernel may reach another device: no remote copies, remote signals or barrier semaphores. Data moves between devices by JAX's collectives and lax.ppermute only.
A program may use at most 128 MiB of HBM per device.

```python
import math
import jax
import jax.numpy as jnp
from jax import lax

MODEL_WIDTH = 1152
SLOTS = 2
NB = 32
SLOT_TOTAL = 64


def draw_gradients(key, part):
    key_noise = jax.random.fold_in(key, 11)
    key_rows = jax.random.fold_in(key, 12)
    key_cols = jax.random.fold_in(key, 13)
    random_noise = jnp.clip(jax.random.normal(key_noise, (NB, MODEL_WIDTH, MODEL_WIDTH), jnp.float32), -4.0, 4.0)
    ramp_top = 3.0
    row_scale = jnp.exp(jax.random.uniform(key_rows, (NB, MODEL_WIDTH, 1), jnp.float32, jnp.log(0.3), jnp.log(3.0)))
    col_scale = jnp.exp(jax.random.uniform(key_cols, (NB, 1, MODEL_WIDTH), jnp.float32, jnp.log(0.5), jnp.log(2.0)))
    column_place = jnp.arange(MODEL_WIDTH, dtype=jnp.float32) / (MODEL_WIDTH - 1.0)
    column_ramp = jnp.exp(column_place * jnp.log(ramp_top))[None, None, :] / ramp_top ** 0.5
    return (random_noise * row_scale * col_scale * column_ramp).astype(jnp.bfloat16)


def draw_owner_list(key, part):
    key_perm = jax.random.fold_in(key, 21)
    key_coin = jax.random.fold_in(key, 22)
    key_order = jax.random.fold_in(key, 23)
    shuffled = jax.random.permutation(key_perm, NB).astype(jnp.int32)
    coins = jax.random.randint(key_coin, (NB // 2,), 0, 2).astype(jnp.int32)
    coins = coins.at[0].set(1)
    positions = jnp.arange(NB, dtype=jnp.int32)
    pair_index = positions // 2
    first_owner = shuffled[2 * pair_index]
    second_owner = shuffled[2 * pair_index + 1]
    odd_place = positions % 2
    chosen = jnp.where(odd_place == 0, first_owner, jnp.where(coins[pair_index] == 1, first_owner, second_owner))
    order = jax.random.permutation(key_order, NB).astype(jnp.int32)
    return jnp.zeros((NB,), jnp.int32).at[order].set(chosen)


def root_matrix(key):
    key_offdiagonal = jax.random.fold_in(key, 31)
    key_diagonal = jax.random.fold_in(key, 32)
    random_noise = jnp.clip(jax.random.normal(key_offdiagonal, (SLOT_TOTAL, MODEL_WIDTH, MODEL_WIDTH), jnp.float32), -5.0, 5.0)
    symmetric = (random_noise + jnp.transpose(random_noise, (0, 2, 1))) * (0.3 / (2.0 * MODEL_WIDTH) ** 0.5)
    diagonal_entries = jnp.exp(jax.random.uniform(key_diagonal, (SLOT_TOTAL, 1, MODEL_WIDTH), jnp.float32, 0.0, jnp.log(3.0)))
    eye_mask = jnp.eye(MODEL_WIDTH, dtype=jnp.bool_)[None, :, :]
    return jnp.where(eye_mask, diagonal_entries, symmetric).astype(jnp.bfloat16)


def draw_left_root(key, part):
    return root_matrix(jax.random.fold_in(key, 41))


def draw_right_root(key, part):
    return root_matrix(jax.random.fold_in(key, 42))


def block_scale(stream_key, dims, split, least, high):
    def one(axis_at, blocks):
        steps = jax.random.uniform(jax.random.fold_in(jax.random.fold_in(stream_key, 6), axis_at), (blocks,), jnp.float32, least / len(split), high / len(split))
        return jnp.repeat(jnp.exp(steps), dims[axis_at] // blocks).reshape((-1,) + (1,) * (len(dims) - axis_at - 1))

    loudness = one(*split[0])
    for cut in split[1:]:
        loudness = loudness * one(*cut)
    return loudness


def gaussian(key, dims, deviation, most, split=(), kind=jnp.bfloat16):
    factor_of = block_scale(key, dims, split, -0.22, 0.18) if split else 1.0
    entries = jax.random.normal(key, dims, jnp.float32) * deviation * factor_of
    return jnp.minimum(jnp.maximum(entries, -most), most).astype(kind)


def setup_inputs(seed: int = 0) -> dict:
    keys = jax.random.split(jax.random.key(seed), 9)
    gradients = draw_gradients(jax.random.fold_in(keys[8], 71), 0)
    weights = gaussian(keys[1], (NB, MODEL_WIDTH, MODEL_WIDTH), MODEL_WIDTH ** -0.5, 0.1875, ((1, 32), (2, 4)), jnp.float32)
    owner_list = draw_owner_list(jax.random.fold_in(keys[8], 71), 0)
    left_gram_stats = gaussian(keys[3], (SLOT_TOTAL, MODEL_WIDTH, MODEL_WIDTH), 1.0, 6.0, ((0, 32), (1, 4)), jnp.float32)
    right_gram_stats = gaussian(keys[4], (SLOT_TOTAL, MODEL_WIDTH, MODEL_WIDTH), 1.0, 6.0, ((0, 32), (1, 4)), jnp.float32)
    left_root = draw_left_root(jax.random.fold_in(keys[8], 71), 0)
    right_root = draw_right_root(jax.random.fold_in(keys[8], 71), 0)
    adam_second_moment = jnp.clip(jnp.exp(math.log(10.0) - 4.6051702 * jax.random.uniform(keys[7], (SLOT_TOTAL, MODEL_WIDTH, MODEL_WIDTH), jnp.float32) ** block_scale(keys[7], (SLOT_TOTAL, MODEL_WIDTH, MODEL_WIDTH), ((0, 32), (2, 4)), -0.2, 0.2)), 0.1, 10.0)
    return dict(gradients=gradients, weights=weights, owner_list=owner_list, left_gram_stats=left_gram_stats, right_gram_stats=right_gram_stats, left_root=left_root, right_root=right_root, adam_second_moment=adam_second_moment)


stat_decay = 0.95
moment_decay = 0.95
learn_rate = 0.02
graft_eps = 1e-06

def slot_table(owner_list):
    count = owner_list.shape[0]
    positions = jnp.arange(count, dtype=jnp.int32)
    earlier = (owner_list[:, None] == owner_list[None, :]) & (positions[None, :] < positions[:, None])
    slot_rank = lax.optimization_barrier(jnp.sum(earlier.astype(jnp.int32), axis=1)).astype(jnp.int32)
    return (slot_rank, (owner_list * SLOTS + slot_rank).astype(jnp.int32))

def reference(gradients, weights, owner_list, left_gram_stats, right_gram_stats, left_root, right_root, adam_second_moment):
    slot_rank, slot_index = slot_table(owner_list)

    def one_block(item):
        block, place = item
        grad_full = block.astype(jnp.float32)
        gram_left = jnp.dot(block, block.T, preferred_element_type=jnp.float32) / MODEL_WIDTH
        gram_right = jnp.dot(block.T, block, preferred_element_type=jnp.float32) / MODEL_WIDTH
        left_new = stat_decay * left_gram_stats[place] + gram_left
        right_new = stat_decay * right_gram_stats[place] + gram_right
        moment_new = moment_decay * adam_second_moment[place] + (1.0 - moment_decay) * grad_full * grad_full
        adam_dir = grad_full / jnp.sqrt(moment_new)
        product = jnp.dot(block, right_root[place], preferred_element_type=jnp.float32).astype(jnp.bfloat16)
        precond = jnp.dot(left_root[place], product, preferred_element_type=jnp.float32)
        ratio = jnp.sqrt(jnp.mean(adam_dir * adam_dir)) / jnp.sqrt(jnp.mean(precond * precond) + graft_eps)
        return (left_new, right_new, moment_new, -learn_rate * ratio * precond)
    left_live, right_live, moment_live, updates = lax.map(one_block, (gradients, slot_index))
    new_left = (stat_decay * left_gram_stats).at[slot_index].set(left_live)
    new_right = (stat_decay * right_gram_stats).at[slot_index].set(right_live)
    new_moment = (moment_decay * adam_second_moment).at[slot_index].set(moment_live)
    new_weights = weights + updates
    return (new_weights, new_left, new_right, new_moment)
```

```python
import jax
import jax.numpy as jnp
from jax import lax
from jax.experimental import pallas as pl
from jax.experimental.pallas import tpu as pltpu
from jax.sharding import PartitionSpec as P

stat_decay = 0.95
moment_decay = 0.95
learn_rate = 0.02
graft_eps = 1e-06

f32 = jnp.float32
bf16 = jnp.bfloat16
VM = pl.BlockSpec(memory_space=pltpu.VMEM)
SM = pl.BlockSpec(memory_space=pltpu.SMEM)
ANY = pl.BlockSpec(memory_space=pl.ANY)

NN = (((1,), (0,)), ((), ()))
NT = (((1,), (1,)), ((), ()))
TN = (((0,), (0,)), ((), ()))


def dot(a, b, dims):
    return lax.dot_general(a, b, dims, preferred_element_type=f32)


def params(mib, **kw):
    return pltpu.CompilerParams(vmem_limit_bytes=mib * 1024 * 1024, **kw)


def cost(flops, nbytes):
    return pl.CostEstimate(flops=int(flops), bytes_accessed=int(nbytes), transcendentals=0)


def fill_slots(owner_ref, table_ref):
    @pl.loop(0, table_ref.shape[0])
    def _(i):
        table_ref[i] = -1

    @pl.loop(0, owner_ref.shape[0])
    def _(b):
        first = 2 * owner_ref[b]
        rank = (table_ref[first] >= 0).astype(jnp.int32)
        table_ref[first + rank] = b


def pick_kernel(rank, owner_ref, grad_ref, out_ref, table_ref, wide_ref):
    fill_slots(owner_ref, table_ref)
    wide_ref[...] = pltpu.einshape("rbc->brc", grad_ref[...].astype(f32))

    @pl.loop(0, out_ref.shape[0])
    def _(d):
        b = table_ref[2 * d + rank]

        @pl.when(b >= 0)
        def _():
            out_ref[d] = wide_ref[b].astype(bf16)

        @pl.when(b < 0)
        def _():
            out_ref[d] = jnp.zeros(out_ref.shape[1:], bf16)


def pick(rank, owner_list, gradients, shards):
    rows, nb, width = gradients.shape
    return pl.pallas_call(
        lambda *refs: pick_kernel(rank, *refs),
        out_shape=jax.ShapeDtypeStruct((shards, rows, width), bf16),
        in_specs=[SM, VM],
        out_specs=VM,
        scratch_shapes=[
            pltpu.SMEM((2 * shards,), jnp.int32),
            pltpu.VMEM((nb, rows, width), f32),
        ],
        compiler_params=params(12),
        cost_estimate=cost(0, 5 * gradients.size),
        name="pick%d" % rank,
    )(owner_list, gradients)


def turn_kernel(got_ref, out_ref, wide_ref):
    count, rows, width = got_ref.shape
    for s in range(count):
        wide_ref[s * rows : (s + 1) * rows, :] = got_ref[s].astype(f32)
    out_ref[...] = wide_ref[...].T.astype(bf16)


def turn(got):
    count, rows, width = got.shape
    return pl.pallas_call(
        turn_kernel,
        out_shape=jax.ShapeDtypeStruct((width, count * rows), bf16),
        in_specs=[VM],
        out_specs=VM,
        scratch_shapes=[pltpu.VMEM((count * rows, width), f32)],
        compiler_params=params(8),
        cost_estimate=cost(0, 5 * got.size),
        name="turn",
    )(got)


def moment_kernel(g0_ref, g1_ref, mom_ref, out_ref, sum_ref):
    for s, part in enumerate((g0_ref, g1_ref)):
        g = part[...].astype(f32)
        v = moment_decay * mom_ref[s] + ((1.0 - moment_decay) * g) * g
        out_ref[s] = v
        d = g / jnp.sqrt(v)
        total = jnp.sum(d * d, keepdims=True)
        sum_ref[s] = jnp.broadcast_to(total, sum_ref.shape[1:])


def moments(parts, mom):
    return pl.pallas_call(
        moment_kernel,
        out_shape=(
            jax.ShapeDtypeStruct(mom.shape, f32),
            jax.ShapeDtypeStruct((2, 8, 128), f32),
        ),
        in_specs=[VM] * 3,
        out_specs=(VM, VM),
        compiler_params=params(16),
        cost_estimate=cost(10 * mom.size, 9 * mom.size),
        name="moments",
    )(*parts, mom)


def lane_block(n):
    return (n + 127) // 128 * 128


def cut_kernel(pos_ref, rows_ref, plus_ref, diag_ref, mid_ref, pad_ref):
    slots, part, wide = rows_ref.shape
    count = wide // part
    gap = pad_ref.shape[1] // count
    pos = pos_ref[0]
    for s in range(slots):
        for k in range(count):
            pad_ref[:, k * gap : k * gap + part] = rows_ref[s, :, k * part : (k + 1) * part]

        def block(step):
            start = pl.multiple_of(lax.rem(pos + step, count) * gap, 128)
            return pad_ref[:, pl.ds(start, gap)][:, :part]

        diag = block(0)
        for j, value in enumerate((block(3), diag, block(2))):
            at = (3 * s + j) * part
            plus_ref[:, at : at + part] = value
        diag_ref[:, s * part : (s + 1) * part] = diag
        mid_ref[:, s * part : (s + 1) * part] = block(1)


def cut(pos, rows):
    slots, part, wide = rows.shape
    two = jax.ShapeDtypeStruct((part, slots * part), bf16)
    return pl.pallas_call(
        cut_kernel,
        out_shape=(jax.ShapeDtypeStruct((part, 3 * slots * part), bf16), two, two),
        in_specs=[SM, VM],
        out_specs=(VM, VM, VM),
        scratch_shapes=[pltpu.VMEM((part, wide // part * lane_block(part)), bf16)],
        compiler_params=params(8),
        cost_estimate=cost(0, 8 * rows.size),
        name="cut",
    )(pos, rows)


def patch_kernel(shards, pos_ref, rows_ref, plus_ref, diag_ref, mid_ref, far_ref, out_ref):
    slots, part, wide = rows_ref.shape
    count = wide // part
    gap = out_ref.shape[2] // count
    tall = out_ref.shape[1] // count
    each = wide // shards
    lift = tall // (part // each)
    pos = pos_ref[0]
    row = lax.broadcasted_iota(jnp.int32, (tall, part), 0)
    col = lax.broadcasted_iota(jnp.int32, (tall, part), 1)
    spot = (col // each) * lift + lax.rem(col, each)
    place = (row == spot).astype(f32).astype(bf16)
    tail = jnp.zeros((tall, gap - part), bf16)
    for s in range(slots):

        def put(a, b, value, flip):
            rows = pl.ds(pl.multiple_of(a * tall, 16), tall)
            got = dot(place, value, NT if flip else NN).astype(bf16)
            at = pl.ds(pl.multiple_of(b * gap, 128), gap)
            out_ref[s, rows, at] = jnp.concatenate([got, tail], axis=1)

        def at(step):
            return lax.rem(pos + step, count)

        for k in range(count):
            own = rows_ref[s, :, k * part : (k + 1) * part]
            put(pos, k, own, False)
            put(k, pos, own, True)
        edge = plus_ref[:, 3 * s * part : (3 * s + 1) * part]
        put(at(3), at(2), edge, False)
        put(at(2), at(3), edge, True)
        put(at(3), at(3), plus_ref[:, (3 * s + 1) * part : (3 * s + 2) * part], False)
        edge = plus_ref[:, (3 * s + 2) * part : (3 * s + 3) * part]
        put(at(3), at(1), edge, False)
        put(at(1), at(3), edge, True)
        mine = slice(s * part, (s + 1) * part)
        put(at(1), at(1), diag_ref[:, mine], False)
        put(at(1), at(2), mid_ref[:, mine], False)
        put(at(2), at(1), mid_ref[:, mine], True)
        put(at(2), at(2), far_ref[:, mine], False)


def patch(pos, shards, rows, plus, diag, mid, far):
    slots, part, wide = rows.shape
    count = wide // part
    lift = (wide // shards + 7) // 8 * 8
    return pl.pallas_call(
        lambda *refs: patch_kernel(shards, *refs),
        out_shape=jax.ShapeDtypeStruct((slots, shards * lift, count * lane_block(part)), bf16),
        in_specs=[SM] + [VM] * 5,
        out_specs=VM,
        compiler_params=params(24),
        cost_estimate=cost(2 * wide * wide * part * slots, 6 * slots * wide * wide),
        name="patch",
    )(pos, rows, plus, diag, mid, far)


def spread(pos, count, parts, full_ref, sems):
    part = parts[0].shape[0]
    half = part // 2
    copies = []
    for i, (piece, step, off) in enumerate(
        zip(parts, (0, count - 1, 1, 2, 2), (0, 0, 0, 0, half))
    ):
        start = pl.multiple_of(lax.rem(pos + step, count) * part + off, 16)
        copies.append(
            pltpu.make_async_copy(piece, full_ref.at[pl.ds(start, piece.shape[0]), :], sems.at[i])
        )
    return copies


def pieces_of(value):
    high = value.astype(bf16).astype(f32)
    mid = (value - high).astype(bf16).astype(f32)
    return high, mid, value - high - mid


def precond_kernel(count, slot, *refs):
    pos_ref, right_ref, adam_ref, root_ref = refs[:4]
    grads = refs[4:9]
    out_ref = refs[9]
    full_ref, root_buf, right_buf, wide_ref, prod_ref, pre_ref, sems = refs[10:]
    first = spread(pos_ref[0], count, grads, full_ref, sems)
    first.append(pltpu.make_async_copy(right_ref.at[slot], right_buf, sems.at[5]))
    second = pltpu.make_async_copy(root_ref.at[slot], root_buf, sems.at[6])
    for c in first:
        c.start()
    second.start()
    part, wide = right_buf.shape
    gap = prod_ref.shape[1] // count
    prod_ref[...] = jnp.zeros(prod_ref.shape, bf16)
    for c in first:
        c.wait()
    step = wide // 3
    for n in range(3):
        cols = slice(n * step, (n + 1) * step)
        wide_ref[:, cols] = dot(right_buf[...], full_ref[:, cols], NN)
    for k in range(count):
        prod_ref[:part, k * gap : k * gap + part] = wide_ref[
            :, k * part : (k + 1) * part
        ].astype(bf16)
    second.wait()
    step = out_ref.shape[0] // 4
    total = jnp.zeros((1, 1), f32)
    for n in range(4):
        rows = slice(n * step, (n + 1) * step)
        got = dot(root_buf[rows, :], prod_ref[...], NT)
        pre_ref[rows, :] = got
        total = total + jnp.sum(got * got, keepdims=True)
    lane = lax.broadcasted_iota(jnp.int32, (step, gap), 1)
    extra = jnp.zeros((step, gap), f32)
    for i, value in enumerate(pieces_of(total) + pieces_of(adam_ref[slot, 0:1, 0:1])):
        extra = jnp.where(lane == part + i, value, extra)
    for n in range(4):
        rows = slice(n * step, (n + 1) * step)
        out_ref[rows, :] = (pre_ref[rows, :] + extra).astype(bf16)


def precondition(pos, count, slot, right, adam, root, grads):
    part, wide = grads[0].shape
    tall, long = root.shape[1:]
    gap = long // count
    return pl.pallas_call(
        lambda *refs: precond_kernel(count, slot, *refs),
        out_shape=jax.ShapeDtypeStruct((tall, gap), bf16),
        in_specs=[SM, ANY, VM, ANY] + [ANY] * 5,
        out_specs=VM,
        scratch_shapes=[
            pltpu.VMEM((wide, wide), bf16),
            pltpu.VMEM((tall, long), bf16),
            pltpu.VMEM((part, wide), bf16),
            pltpu.VMEM((part, wide), f32),
            pltpu.VMEM((gap, long), bf16),
            pltpu.VMEM((tall, gap), f32),
            pltpu.SemaphoreType.DMA((7,)),
        ],
        compiler_params=params(24),
        cost_estimate=cost(4 * part * wide * wide, 4 * wide * wide),
        name="precond%d" % slot,
    )(pos, right, adam, root, *grads)


def gram_kernel(count, *refs):
    pos_ref, left_ref, right_ref = refs[:3]
    grads = (refs[3:8], refs[8:13])
    outl_ref, outr_ref = refs[13:15]
    full_ref, own_ref, sems = refs[15:]
    slot, n = pl.program_id(0), pl.program_id(1)
    pos = pos_ref[0]
    wide = full_ref.shape[1]
    part = own_ref.shape[1]
    step = outl_ref.shape[2]

    def copies(s):
        return spread(pos, count, grads[s], full_ref.at[s], sems.at[s])

    @pl.when((slot == 0) & (n == 0))
    def _():
        for s in range(2):
            for c in copies(s):
                c.start()

    for s in range(2):

        @pl.when((slot == s) & (n == 0))
        def _():
            for c in copies(s):
                c.wait()
            for k in range(count):

                @pl.when(pos == k)
                def _():
                    own_ref[...] = full_ref[s, :, k * part : (k + 1) * part]

    cols = pl.ds(pl.multiple_of(n * step, 128), step)
    left = dot(own_ref[...], full_ref[slot, :, cols], TN)
    outl_ref[0] = stat_decay * left_ref[0] + left / wide
    mine = full_ref[slot, pl.ds(pl.multiple_of(pos * part, 16), part), :]
    right = dot(mine, full_ref[slot, cols, :], NT)
    outr_ref[0] = stat_decay * right_ref[0] + right / wide


def grams(pos, count, left, right, grads0, grads1):
    slots, part, wide = left.shape
    step = wide // 3
    block = pl.BlockSpec((1, part, step), lambda s, n: (s, 0, n))
    return pl.pallas_call(
        lambda *refs: gram_kernel(count, *refs),
        grid=(slots, 3),
        out_shape=(
            jax.ShapeDtypeStruct(left.shape, f32),
            jax.ShapeDtypeStruct(right.shape, f32),
        ),
        in_specs=[SM, block, block] + [ANY] * 10,
        out_specs=(block, block),
        scratch_shapes=[
            pltpu.VMEM((slots, wide, wide), bf16),
            pltpu.VMEM((wide, part), bf16),
            pltpu.SemaphoreType.DMA((slots, 5)),
        ],
        compiler_params=params(24),
        cost_estimate=cost(4 * slots * part * wide * wide, 20 * slots * part * wide),
        name="grams",
    )(pos, left, right, *grads0, *grads1)


def sums_kernel(part, back0_ref, back1_ref, out_ref):
    rows = lax.broadcasted_iota(jnp.int32, out_ref.shape[1:], 0)
    lane = lax.broadcasted_iota(jnp.int32, out_ref.shape[1:], 1)
    for slot, back in enumerate((back0_ref, back1_ref)):
        first = back[:, 0:1, :].astype(f32)
        first = first.reshape(back.shape[0], back.shape[2])

        def value(i):
            at = part + i
            return first[:, at : at + 1] + first[:, at + 1 : at + 2] + first[:, at + 2 : at + 3]

        out_ref[slot] = jnp.where(lane == 0, value(0), jnp.where(lane == 1, value(3), 0.0))


def partial_sums(part, back0, back1):
    return pl.pallas_call(
        lambda *refs: sums_kernel(part, *refs),
        out_shape=jax.ShapeDtypeStruct((2, back0.shape[0], 128), f32),
        in_specs=[VM, VM],
        out_specs=VM,
        compiler_params=params(8),
        name="sums",
    )(back0, back1)


def final_kernel(entries, owner_ref, *refs):
    s0_ref, s1_ref, s2_ref, s3_ref, back0_ref, back1_ref, w_ref = refs[:7]
    out_ref, table_ref, factor_ref, wide_ref = refs[7:]
    fill_slots(owner_ref, table_ref)
    total = s0_ref[...] + s1_ref[...] + s2_ref[...] + s3_ref[...]
    pre_mean = total[:, :, 0:1] / entries
    adam_mean = total[:, :, 1:2] / entries
    factor = -learn_rate * (jnp.sqrt(adam_mean) / jnp.sqrt(pre_mean + graft_eps))
    factor_ref[...] = jnp.broadcast_to(factor, factor_ref.shape)
    rows, nb, part = w_ref.shape

    @pl.loop(0, back0_ref.shape[0])
    def _(d):
        for rank, back_ref in enumerate((back0_ref, back1_ref)):
            b = table_ref[2 * d + rank]

            @pl.when(b >= 0)
            def _():
                scale = factor_ref[rank, pl.ds(d, 1), 0:1]
                wide_ref[b] = scale * back_ref[d, :, :part].astype(f32)

    moved = pltpu.einshape("brc->rbc", wide_ref[...])
    out_ref[...] = w_ref[...] + moved[:rows]


def final(owner_list, sums, backs, weights, entries):
    rows, nb, part = weights.shape
    return pl.pallas_call(
        lambda *refs: final_kernel(entries, *refs),
        out_shape=jax.ShapeDtypeStruct(weights.shape, f32),
        in_specs=[SM] + [VM] * 7,
        out_specs=VM,
        scratch_shapes=[
            pltpu.SMEM((2 * backs[0].shape[0],), jnp.int32),
            pltpu.VMEM((2, backs[0].shape[0], 128), f32),
            pltpu.VMEM((nb, backs[0].shape[1], part), f32),
        ],
        compiler_params=params(20),
        name="final",
    )(owner_list, *sums, *backs, weights)


def body(gradients, weights, owner_list, left_stats, right_stats, left_root, right_root, moment):
    shards = lax.axis_size("shard")
    count = lax.axis_size("tensor")
    pos = lax.axis_index("tensor").astype(jnp.int32).reshape(1)
    up = [(i, (i + 1) % count) for i in range(count)]
    down = [(i, (i - 1) % count) for i in range(count)]

    def ring(a):
        half = a.shape[0] // 2
        l, r = lax.ppermute(a, "tensor", up), lax.ppermute(a, "tensor", down)
        oa = lax.ppermute(l[:half], "tensor", up)
        ob = lax.ppermute(r[half:], "tensor", down)
        return (a, l, r, oa, ob)

    left_rows = jnp.swapaxes(left_root, 1, 2)
    right_rows = jnp.swapaxes(right_root, 1, 2)
    grad_rows = jnp.swapaxes(gradients, 0, 1)
    part, wide = left_rows.shape[1:]

    plus, diag, mid = cut(pos, left_rows)
    plus = lax.ppermute(plus, "tensor", up)
    diag, mid = lax.ppermute(diag, "tensor", down), lax.ppermute(mid, "tensor", down)
    far = lax.ppermute(diag, "tensor", down)

    parts, grads = [], []
    for s in range(2):
        send = pick(s, owner_list, grad_rows, shards)
        got = lax.all_to_all(send, "shard", 0, 0, tiled=True)
        parts.append(turn(got))
        grads.append(ring(parts[s]))
    new_moment, adam = moments(parts, jnp.swapaxes(moment, 1, 2))
    root = patch(pos, shards, left_rows, plus, diag, mid, far)
    backs = []
    for s in range(2):
        update = precondition(pos, count, s, right_rows, adam, root, grads[s])
        update = update.reshape(shards, -1, update.shape[1])
        backs.append(lax.all_to_all(update, "shard", 0, 0, tiled=True))
    new_left, new_right = grams(pos, count, left_stats, right_stats, grads[0], grads[1])
    mine = partial_sums(part, backs[0], backs[1])
    sums = [mine] + [
        lax.ppermute(mine, "tensor", [(i, (i + k) % count) for i in range(count)])
        for k in (1, 2, 3)
    ]
    new_weights = final(
        owner_list, sums, backs, jnp.swapaxes(weights, 0, 1), float(wide * wide)
    )
    return (
        jnp.swapaxes(new_weights, 0, 1),
        new_left,
        new_right,
        jnp.swapaxes(new_moment, 1, 2),
    )


def solution(mesh):
    return jax.shard_map(
        body,
        mesh=mesh,
        in_specs=(
            P(None, "shard", "tensor"),
            P(None, "shard", "tensor"),
            P(),
            P("shard", "tensor", None),
            P("shard", "tensor", None),
            P("shard", None, "tensor"),
            P("shard", None, "tensor"),
            P("shard", None, "tensor"),
        ),
        out_specs=(
            P(None, "shard", "tensor"),
            P("shard", "tensor", None),
            P("shard", "tensor", None),
            P("shard", None, "tensor"),
        ),
        check_vma=False,
    )
```

```python
import jax
import jax.numpy as jnp
from jax import lax
from jax.experimental import pallas as pl
from jax.experimental.pallas import tpu as pltpu
from jax.sharding import PartitionSpec as P


stat_decay = 0.95
moment_decay = 0.95
learn_rate = 0.02
graft_eps = 1e-06

f32 = jnp.float32
bf16 = jnp.bfloat16
VM = pl.BlockSpec(memory_space=pltpu.VMEM)
SM = pl.BlockSpec(memory_space=pltpu.SMEM)
HB = pl.BlockSpec(memory_space=pltpu.HBM)

NN = (((1,), (0,)), ((), ()))
NT = (((1,), (1,)), ((), ()))
TN = (((0,), (0,)), ((), ()))


def dot(a, b, dims):
    return lax.dot_general(a, b, dims, preferred_element_type=f32)


WHOLE = 63


def params(mib, **kw):
    return pltpu.CompilerParams(vmem_limit_bytes=mib * 1024 * 1024, **kw)


def cost(flops, nbytes):
    return pl.CostEstimate(flops=int(flops), bytes_accessed=int(nbytes), transcendentals=0)


def fill_slots(owner_ref, table_ref):
    @pl.loop(0, table_ref.shape[0])
    def _(i):
        table_ref[i] = -1

    @pl.loop(0, owner_ref.shape[0])
    def _(b):
        first = 2 * owner_ref[b]
        rank = (table_ref[first] >= 0).astype(jnp.int32)
        table_ref[first + rank] = b


def pick_kernel(rank, owner_ref, grad_ref, out_hbm, table_ref, wide_ref, out_ref, sem):
    fill_slots(owner_ref, table_ref)
    wide_ref[...] = pltpu.einshape("rbc->brc", grad_ref[...].astype(f32))

    @pl.loop(0, out_ref.shape[0])
    def _(d):
        b = table_ref[2 * d + rank]

        @pl.when(b >= 0)
        def _():
            out_ref[d] = wide_ref[b].astype(bf16)

        @pl.when(b < 0)
        def _():
            out_ref[d] = jnp.zeros(out_ref.shape[1:], bf16)

    pltpu.make_async_copy(out_ref, out_hbm, sem).start()
    pltpu.make_async_copy(out_ref, out_hbm, sem).wait()


def pick(rank, owner_list, gradients, shards):
    rows, nb, width = gradients.shape
    return pl.pallas_call(
        lambda *refs: pick_kernel(rank, *refs),
        out_shape=jax.ShapeDtypeStruct((shards, rows, width), bf16),
        in_specs=[SM, VM],
        out_specs=HB,
        scratch_shapes=[
            pltpu.SMEM((2 * shards,), jnp.int32),
            pltpu.VMEM((nb, rows, width), f32),
            pltpu.VMEM((shards, rows, width), bf16),
            pltpu.SemaphoreType.DMA,
        ],
        compiler_params=params(WHOLE),
        cost_estimate=cost(0, 5 * gradients.size),
    )(owner_list, gradients)


def turn_kernel(got_ref, out_hbm, wide_ref, out_ref, sem):
    count, rows, _ = got_ref.shape
    for s in range(count):
        wide_ref[s * rows : (s + 1) * rows, :] = got_ref[s].astype(f32)
    out_ref[...] = wide_ref[...].T.astype(bf16)
    pltpu.make_async_copy(out_ref, out_hbm, sem).start()
    pltpu.make_async_copy(out_ref, out_hbm, sem).wait()


def turn(got):
    count, rows, width = got.shape
    return pl.pallas_call(
        turn_kernel,
        out_shape=jax.ShapeDtypeStruct((width, count * rows), bf16),
        in_specs=[VM],
        out_specs=HB,
        scratch_shapes=[
            pltpu.VMEM((count * rows, width), f32),
            pltpu.VMEM((width, count * rows), bf16),
            pltpu.SemaphoreType.DMA,
        ],
        compiler_params=params(WHOLE),
        cost_estimate=cost(0, 5 * got.size),
        name="turn",
    )(got)


def moment_kernel(slot, grad_ref, mom_ref, *refs):
    out_ref, sum_ref = refs[slot:]
    g = grad_ref[...].astype(f32)
    v = moment_decay * mom_ref[0] + ((1.0 - moment_decay) * g) * g
    out_ref[0] = v
    d = g * lax.rsqrt(v)
    sum_ref[...] = jnp.broadcast_to(jnp.sum(d * d, keepdims=True), sum_ref.shape)


def moments(slot, grad, mom, before=()):
    _, part, wide = mom.shape
    block = pl.BlockSpec((1, part, wide), lambda n: (slot, 0, 0))
    return pl.pallas_call(
        lambda *refs: moment_kernel(slot, *refs),
        grid=(1,),
        out_shape=(
            jax.ShapeDtypeStruct(mom.shape, f32),
            jax.ShapeDtypeStruct((8, 128), f32),
        ),
        in_specs=[pl.BlockSpec((part, wide), lambda n: (0, 0)), block] + [HB] * len(before),
        out_specs=(block, pl.BlockSpec((8, 128), lambda n: (0, 0))),
        input_output_aliases={2 + i: i for i in range(len(before))},
        compiler_params=params(WHOLE),
        cost_estimate=cost(5 * mom.size, 5 * mom.size),
    )(grad, mom, *before)


def lane_block(n):
    return (n + 127) // 128 * 128


def cut_kernel(pos_ref, rows_ref, plus_ref, minus_ref, pad_ref):
    slots, part, wide = rows_ref.shape
    count = wide // part
    gap = pad_ref.shape[1] // count
    pos = pos_ref[0]
    for s in range(slots):
        for k in range(count):
            pad_ref[:, k * gap : k * gap + part] = rows_ref[s, :, k * part : (k + 1) * part]

        def block(step):
            start = pl.multiple_of(lax.rem(pos + step, count) * gap, 128)
            return pad_ref[:, pl.ds(start, gap)][:, :part]

        diag = block(0)
        for j, value in enumerate((block(3), diag, block(2))):
            at = (3 * s + j) * part
            plus_ref[:, at : at + part] = value
        mine = slice(s * part, (s + 1) * part)
        minus_ref[:part, mine] = diag
        minus_ref[part:, mine] = block(1)


def cut(pos, rows):
    slots, part, wide = rows.shape
    return pl.pallas_call(
        cut_kernel,
        out_shape=(
            jax.ShapeDtypeStruct((part, 3 * slots * part), bf16),
            jax.ShapeDtypeStruct((2 * part, slots * part), bf16),
        ),
        in_specs=[SM, VM],
        out_specs=(VM, VM),
        scratch_shapes=[pltpu.VMEM((part, wide // part * lane_block(part)), bf16)],
        compiler_params=params(WHOLE),
        cost_estimate=cost(0, 8 * rows.size),
        name="cut",
    )(pos, rows)


def patch_kernel(shards, s, pos_ref, rows_ref, plus_ref, minus_ref, far_ref, out_hbm, out_ref, sem):
    part, wide = rows_ref.shape[1:]
    count = wide // part
    gap = out_ref.shape[1] // count
    each = wide // shards
    pos = pos_ref[0]
    row = lax.broadcasted_iota(jnp.int32, (part, gap), 0)
    col = lax.broadcasted_iota(jnp.int32, (part, gap), 1)
    place = (col == (row // each) * lifted(each) + lax.rem(row, each)).astype(f32).astype(bf16)

    def put(a, b, value, flip):
        rows = pl.ds(pl.multiple_of(a * part, 16), part)
        at = pl.ds(pl.multiple_of(b * gap, 128), gap)
        out_ref[rows, at] = dot(value, place, TN if flip else NN).astype(bf16)

    def at(step):
        return lax.rem(pos + step, count)

    for k in range(count):
        own = rows_ref[0, :, k * part : (k + 1) * part]
        put(pos, k, own, False)
        put(k, pos, own, True)
    edge = plus_ref[:, 3 * s * part : (3 * s + 1) * part]
    put(at(3), at(2), edge, False)
    put(at(2), at(3), edge, True)
    put(at(3), at(3), plus_ref[:, (3 * s + 1) * part : (3 * s + 2) * part], False)
    edge = plus_ref[:, (3 * s + 2) * part : (3 * s + 3) * part]
    put(at(3), at(1), edge, False)
    put(at(1), at(3), edge, True)
    mine = slice(s * part, (s + 1) * part)
    put(at(1), at(1), minus_ref[:part, mine], False)
    put(at(1), at(2), minus_ref[part:, mine], False)
    put(at(2), at(1), minus_ref[part:, mine], True)
    put(at(2), at(2), far_ref[:, mine], False)
    copy = pltpu.make_async_copy(out_ref, out_hbm, sem)
    copy.start()
    copy.wait()


def lifted(n):
    return (n + 7) // 8 * 8


def patch(slot, pos, shards, rows, plus, minus, far):
    _, part, wide = rows.shape
    count = wide // part
    gap = lane_block(shards // count * lifted(wide // shards))
    shape = (wide, count * gap)

    def whole(x):
        return pl.BlockSpec(x.shape, lambda n: (0, 0))

    return pl.pallas_call(
        lambda *refs: patch_kernel(shards, slot, *refs),
        grid=(1,),
        out_shape=jax.ShapeDtypeStruct(shape, bf16),
        in_specs=[
            SM,
            pl.BlockSpec((1, part, wide), lambda n: (slot, 0, 0)),
            whole(plus),
            whole(minus),
            whole(far),
        ],
        out_specs=HB,
        scratch_shapes=[pltpu.VMEM(shape, bf16), pltpu.SemaphoreType.DMA],
        compiler_params=params(WHOLE),
        cost_estimate=cost(wide * wide * part, 3 * wide * wide),
    )(pos, rows, plus, minus, far)


def spread(pos, count, parts, full_ref, sems):
    part = parts[0].shape[0]
    copies = []
    for i, (piece, step) in enumerate(zip(parts, (0, count - 1, 1, 2))):
        start = pl.multiple_of(lax.rem(pos + step, count) * part, 16)
        copies.append(
            pltpu.make_async_copy(piece, full_ref.at[pl.ds(start, part), :], sems.at[i])
        )
    return copies


def pieces_of(value):
    high = value.astype(bf16).astype(f32)
    rest = jnp.where(high < 3e38, value - high, 0.0)
    mid = rest.astype(bf16).astype(f32)
    return high, mid, rest - mid


def precond_kernel(count, slot, *refs):
    pos_ref, right_ref, adam_ref, root_ref = refs[:4]
    grads = refs[4:8]
    out_hbm = refs[8]
    full_ref, root_buf, right_buf, prod_ref, pre_ref, out_ref, sems = refs[9:]
    first = spread(pos_ref[0], count, grads, full_ref, sems)
    first.append(pltpu.make_async_copy(right_ref.at[slot], right_buf, sems.at[4]))
    second = pltpu.make_async_copy(root_ref, root_buf, sems.at[5])
    for c in first:
        c.start()
    second.start()
    part, wide = right_buf.shape
    gap = root_buf.shape[1] // count
    for c in first:
        c.wait()
    step = wide // 3
    for n in range(3):
        cols = slice(n * step, (n + 1) * step)
        prod_ref[:, cols] = dot(right_buf[...], full_ref[:, cols], NN).astype(bf16)
    second.wait()
    total = jnp.zeros((1, 1), f32)
    for k in range(count):
        got = dot(prod_ref[...], root_buf[:, k * gap : (k + 1) * gap], NN)
        pre_ref[k] = got
        total = total + jnp.sum(got * got, keepdims=True)
    used, lanes = out_ref.shape[1:]
    rows = lax.broadcasted_iota(jnp.int32, (lanes - part, used), 0)
    extra = jnp.zeros((lanes - part, used), f32)
    for i, value in enumerate(pieces_of(total) + pieces_of(adam_ref[0:1, 0:1])):
        extra = jnp.where(rows == i, value, extra)
    for k in range(count):
        both = jnp.concatenate([pre_ref[k][:, :used], extra], axis=0)
        out_ref[k] = both.T.astype(bf16)
    last = pltpu.make_async_copy(out_ref, out_hbm, sems.at[0])
    last.start()
    last.wait()


def precondition(pos, count, shards, slot, right, adam, root, grads):
    part, wide = grads[0].shape
    long = root.shape[1]
    gap = long // count
    used = shards // count * lifted(wide // shards)
    lanes = lane_block(part)
    return pl.pallas_call(
        lambda *refs: precond_kernel(count, slot, *refs),
        out_shape=jax.ShapeDtypeStruct((count, used, lanes), bf16),
        in_specs=[SM, HB, VM, HB] + [HB] * 4,
        out_specs=HB,
        scratch_shapes=[
            pltpu.VMEM((wide, wide), bf16),
            pltpu.VMEM((wide, long), bf16),
            pltpu.VMEM((part, wide), bf16),
            pltpu.VMEM((part, wide), bf16),
            pltpu.VMEM((count, part, gap), f32),
            pltpu.VMEM((count, used, lanes), bf16),
            pltpu.SemaphoreType.DMA((6,)),
        ],
        compiler_params=params(WHOLE),
        cost_estimate=cost(4 * part * wide * wide, 4 * wide * wide),
    )(pos, right, adam, root, *grads)


def gram_kernel(count, slot, *refs):
    pos_ref, left_ref, right_ref = refs[:3]
    grads = refs[3:7]
    outl_ref, outr_ref, full_ref, own_ref, sems = refs[7 + 2 * slot :]
    n = pl.program_id(0)
    pos = pos_ref[0]
    wide = full_ref.shape[1]
    part = own_ref.shape[1]
    step = outl_ref.shape[2]

    @pl.when(n == 0)
    def _():
        copies = spread(pos, count, grads, full_ref, sems)
        for c in copies:
            c.start()
        for c in copies:
            c.wait()
        for k in range(count):

            @pl.when(pos == k)
            def _():
                own_ref[...] = full_ref[:, k * part : (k + 1) * part]

    cols = pl.ds(pl.multiple_of(n * step, 128), step)
    left = dot(own_ref[...], full_ref[:, cols], TN)
    outl_ref[0] = stat_decay * left_ref[0] + left / wide
    mine = full_ref[pl.ds(pl.multiple_of(pos * part, 16), part), :]
    right = dot(mine, full_ref[cols, :], NT)
    outr_ref[0] = stat_decay * right_ref[0] + right / wide


def grams(pos, count, slot, left, right, grads, before=()):
    _, part, wide = left.shape
    step = wide // 3
    block = pl.BlockSpec((1, part, step), lambda n: (slot, 0, n))
    shape = jax.ShapeDtypeStruct(left.shape, f32)
    return pl.pallas_call(
        lambda *refs: gram_kernel(count, slot, *refs),
        grid=(3,),
        out_shape=(shape, shape),
        in_specs=[SM, block, block] + [HB] * (4 + len(before)),
        out_specs=(block, block),
        scratch_shapes=[
            pltpu.VMEM((wide, wide), bf16),
            pltpu.VMEM((wide, part), bf16),
            pltpu.SemaphoreType.DMA((4,)),
        ],
        input_output_aliases={7 + i: i for i in range(len(before))},
        compiler_params=params(WHOLE),
        cost_estimate=cost(4 * part * wide * wide, 20 * part * wide),
    )(pos, left, right, *grads, *before)


def sums_kernel(at, back0_ref, back1_ref, out_ref):
    shards, _, lanes = back0_ref.shape
    lane = lax.broadcasted_iota(jnp.int32, (shards, lanes), 1)
    kept = jnp.zeros((shards, lanes), f32)
    for slot, back in enumerate((back0_ref, back1_ref)):
        first = back[...].astype(f32)[:, 0, :]
        for i in range(2):
            terms = [first[:, at + 3 * i + j : at + 3 * i + j + 1] for j in range(3)]
            kept = jnp.where(lane == 2 * slot + i, terms[0] + terms[1] + terms[2], kept)
    out_ref[...] = jnp.concatenate([kept.T[:8], jnp.zeros((8, lanes - shards), f32)], axis=1)


def partial_sums(part, back0, back1):
    shards = back0.shape[0]
    block = pl.BlockSpec((shards, 8, 128), lambda n: (0, 0, part // 128))
    return pl.pallas_call(
        lambda *refs: sums_kernel(part % 128, *refs),
        grid=(1,),
        out_shape=jax.ShapeDtypeStruct((8, 128), f32),
        in_specs=[block, block],
        out_specs=pl.BlockSpec((8, 128), lambda n: (0, 0)),
        compiler_params=params(8),
        name="sums",
    )(back0, back1)


def place_kernel(owner_ref, back0_ref, back1_ref, out_ref, where_ref, table_ref, wide_ref):
    fill_slots(owner_ref, table_ref)
    rows, _, part = out_ref.shape
    lane = lax.broadcasted_iota(jnp.int32, (1, where_ref.shape[2]), 1)
    where_ref[...] = jnp.zeros(where_ref.shape, f32)

    @pl.loop(0, back0_ref.shape[0])
    def _(d):
        for rank, back_ref in enumerate((back0_ref, back1_ref)):
            b = table_ref[2 * d + rank]

            @pl.when(b >= 0)
            def _():
                wide_ref[b] = back_ref[d, :, :part].astype(f32)
                where_ref[rank, pl.ds(b, 1), :] = (lane == d).astype(f32)

    out_ref[...] = pltpu.einshape("brc->rbc", wide_ref[...])[:rows]


def place(owner_list, backs, rows, part):
    nb = owner_list.shape[0]
    shards, lift = backs[0].shape[:2]
    return pl.pallas_call(
        place_kernel,
        out_shape=(
            jax.ShapeDtypeStruct((rows, nb, part), f32),
            jax.ShapeDtypeStruct((2, nb, 128), f32),
        ),
        in_specs=[SM, VM, VM],
        out_specs=(VM, VM),
        scratch_shapes=[
            pltpu.SMEM((2 * shards,), jnp.int32),
            pltpu.VMEM((nb, lift, part), f32),
        ],
        compiler_params=params(8),
        cost_estimate=cost(0, 8 * rows * nb * part),
        name="place",
    )(owner_list, *backs)


def final_kernel(entries, s0_ref, s1_ref, where_ref, dir_ref, w_ref, out_ref):
    total = (s0_ref[...] + s1_ref[...]) / entries

    def factor(rank):
        pre_mean, adam_mean = total[2 * rank : 2 * rank + 1], total[2 * rank + 1 : 2 * rank + 2]
        return -learn_rate * (jnp.sqrt(adam_mean) / jnp.sqrt(pre_mean + graft_eps))

    chosen = where_ref[0] * factor(0) + where_ref[1] * factor(1)
    scale = jnp.sum(chosen, axis=1, keepdims=True)
    for r in range(out_ref.shape[0]):
        out_ref[r] = w_ref[r] + scale * dir_ref[r]


def final(sums, where, direction, weights, entries):
    return pl.pallas_call(
        lambda *refs: final_kernel(entries, *refs),
        out_shape=jax.ShapeDtypeStruct(weights.shape, f32),
        in_specs=[VM] * 5,
        out_specs=VM,
        compiler_params=params(8),
        name="final",
    )(*sums, where, direction, weights)


def step(gradients, weights, owner_list, left_stats, right_stats, left_root, right_root, moment):
    shards = lax.axis_size("shard")
    count = lax.axis_size("tensor")
    pos = lax.axis_index("tensor").astype(jnp.int32).reshape(1)

    def shift(x, by):
        ring = [(i, (i + by) % count) for i in range(count)]
        return lax.ppermute(x, "tensor", ring)

    def exchange(x):
        return lax.all_to_all(x, "shard", 0, 0, tiled=True)

    left_rows = jnp.swapaxes(left_root, 1, 2)
    right_rows = jnp.swapaxes(right_root, 1, 2)
    grad_rows = jnp.swapaxes(gradients, 0, 1)
    mom_rows = jnp.swapaxes(moment, 1, 2)
    part, wide = left_rows.shape[1:]

    plus, minus = cut(pos, left_rows)
    plus, minus = shift(plus, 1), shift(minus, -1)
    far = shift(minus[:part], -1)

    parts, grads = [], []
    for s in range(2):
        send = pick(s, owner_list, grad_rows, shards)
        own = turn(exchange(send))
        l, r = shift(own, 1), shift(own, -1)
        far_part = shift(l, 1) if s == 0 else shift(r, -1)
        parts.append(own)
        grads.append((own, l, r, far_part))
    before, roots, adams, backs = (), [], [], []
    for s in range(2):
        new_moment, adam = moments(s, parts[s], mom_rows, before)
        before = (new_moment,)
        adams.append(adam)
        roots.append(patch(s, pos, shards, left_rows, plus, minus, far))
    for s in range(2):
        update = precondition(pos, count, shards, s, right_rows, adams[s], roots[s], grads[s])
        backs.append(exchange(update.reshape(shards, -1, update.shape[2])))
    stats = ()
    for s in range(2):
        stats = grams(pos, count, s, left_stats, right_stats, grads[s], stats)
    new_left, new_right = stats
    mine = partial_sums(part, backs[0], backs[1])

    def swap(x, flip):
        pairs = [(i, i ^ flip) for i in range(count)]
        return lax.ppermute(x, "tensor", pairs)

    mine = mine + swap(mine, 1)
    sums = [mine, swap(mine, 3)]
    rows = weights.shape[1]
    direction, where = place(owner_list, backs, rows, part)
    w_rows = jnp.swapaxes(weights, 0, 1)
    new_weights = final(sums, where, direction, w_rows, float(wide * wide))
    return (
        jnp.swapaxes(new_weights, 0, 1),
        new_left,
        new_right,
        jnp.swapaxes(new_moment, 1, 2),
    )


def solution(mesh):
    return jax.shard_map(
        step,
        mesh=mesh,
        in_specs=(
            P(None, "shard", "tensor"),
            P(None, "shard", "tensor"),
            P(),
            P("shard", "tensor", None),
            P("shard", "tensor", None),
            P("shard", None, "tensor"),
            P("shard", None, "tensor"),
            P("shard", None, "tensor"),
        ),
        out_specs=(
            P(None, "shard", "tensor"),
            P("shard", "tensor", None),
            P("shard", "tensor", None),
            P("shard", None, "tensor"),
        ),
        check_vma=False,
    )
```

```python
import jax
import jax.numpy as jnp
from jax import lax
from jax.experimental import pallas as pl
from jax.experimental.pallas import tpu as pltpu
from jax.sharding import PartitionSpec as P


stat_decay = 0.95
moment_decay = 0.95
learn_rate = 0.02
graft_eps = 1e-06

f32 = jnp.float32
bf16 = jnp.bfloat16
VM = pl.BlockSpec(memory_space=pltpu.VMEM)
SM = pl.BlockSpec(memory_space=pltpu.SMEM)
HB = pl.BlockSpec(memory_space=pltpu.HBM)

NN = (((1,), (0,)), ((), ()))
NT = (((1,), (1,)), ((), ()))
TN = (((0,), (0,)), ((), ()))


def dot(a, b, dims):
    return lax.dot_general(a, b, dims, preferred_element_type=f32)


WHOLE = 63


def params(mib, **kw):
    return pltpu.CompilerParams(vmem_limit_bytes=mib * 1024 * 1024, **kw)


def cost(flops, nbytes):
    return pl.CostEstimate(flops=int(flops), bytes_accessed=int(nbytes), transcendentals=0)


def fill_slots(owner_ref, table_ref):
    @pl.loop(0, table_ref.shape[0])
    def _(i):
        table_ref[i] = -1

    @pl.loop(0, owner_ref.shape[0])
    def _(b):
        first = 2 * owner_ref[b]
        rank = (table_ref[first] >= 0).astype(jnp.int32)
        table_ref[first + rank] = b


PACKED = 88


def pack(x, extra=None):
    row = lax.broadcasted_iota(jnp.int32, (8, 128), 0)
    lane = lax.broadcasted_iota(jnp.int32, (8, 128), 1)
    tail = x[:, 256:384]
    wrapped = tail[0:8]
    for j in range(1, 4):
        turned = pltpu.roll(tail[8 * j : 8 * j + 8], 32 * j, 1)
        wrapped = jnp.where(lane >= 32 * j, turned, wrapped)
    low = jnp.where(row < 4, x[32:40, 0:128], pltpu.roll(x[32:40, 128:256], 4, 0))
    last = tail[32:40] if extra is None else jnp.where(lane < 32, tail[32:40], extra)
    return jnp.concatenate([x[0:32, 0:128], x[0:32, 128:256], wrapped, low, last], axis=0)


def unpack(y, put):
    put(0, 0, y[0:32])
    put(0, 128, y[32:64])
    for j in range(4):
        part = y[64:72] if j == 0 else pltpu.roll(y[64:72], 128 - 32 * j, 1)
        put(8 * j, 256, part[:, :32])
    put(32, 0, y[72:76])
    put(32, 128, pltpu.roll(y[72:80], 4, 0)[0:4])
    put(32, 256, y[80:84, :32])


def pick_kernel(rank, owner_ref, grad_ref, out_hbm, table_ref, wide_ref, out_ref, sem):
    fill_slots(owner_ref, table_ref)
    rows, _, width = grad_ref.shape
    wide_ref[:, :rows, :width] = pltpu.einshape("rbc->brc", grad_ref[...].astype(f32))

    @pl.loop(0, out_ref.shape[0])
    def _(d):
        b = table_ref[2 * d + rank]

        @pl.when(b >= 0)
        def _():
            out_ref[d] = pack(wide_ref[b]).astype(bf16)

        @pl.when(b < 0)
        def _():
            out_ref[d] = jnp.zeros(out_ref.shape[1:], bf16)

    pltpu.make_async_copy(out_ref, out_hbm, sem).start()
    pltpu.make_async_copy(out_ref, out_hbm, sem).wait()


def pick(rank, owner_list, gradients, shards):
    _, nb, _ = gradients.shape
    return pl.pallas_call(
        lambda *refs: pick_kernel(rank, *refs),
        out_shape=jax.ShapeDtypeStruct((shards, PACKED, 128), bf16),
        in_specs=[SM, VM],
        out_specs=HB,
        scratch_shapes=[
            pltpu.SMEM((2 * shards,), jnp.int32),
            pltpu.VMEM((nb, 40, 384), f32),
            pltpu.VMEM((shards, PACKED, 128), bf16),
            pltpu.SemaphoreType.DMA,
        ],
        compiler_params=params(WHOLE),
        cost_estimate=cost(0, 5 * gradients.size),
    )(owner_list, gradients)


def turn_kernel(got_ref, out_hbm, wide_ref, out_ref, sem):
    count = got_ref.shape[0]
    rows = wide_ref.shape[0] // count
    for s in range(count):

        def put(row, column, value):
            at = s * rows + row
            wide_ref[at : at + value.shape[0], column : column + value.shape[1]] = value

        unpack(got_ref[s].astype(f32), put)
    out_ref[...] = wide_ref[...].T.astype(bf16)
    pltpu.make_async_copy(out_ref, out_hbm, sem).start()
    pltpu.make_async_copy(out_ref, out_hbm, sem).wait()


def turn(got, rows, width):
    count = got.shape[0]
    return pl.pallas_call(
        turn_kernel,
        out_shape=jax.ShapeDtypeStruct((width, count * rows), bf16),
        in_specs=[VM],
        out_specs=HB,
        scratch_shapes=[
            pltpu.VMEM((count * rows, width), f32),
            pltpu.VMEM((width, count * rows), bf16),
            pltpu.SemaphoreType.DMA,
        ],
        compiler_params=params(8),
        cost_estimate=cost(0, 5 * got.size),
        name="turn",
    )(got)


def moment_kernel(slot, grad_ref, mom_ref, *refs):
    out_ref, sum_ref = refs[slot:]
    g = grad_ref[...].astype(f32)
    v = moment_decay * mom_ref[0] + ((1.0 - moment_decay) * g) * g
    out_ref[0] = v
    d = g * lax.rsqrt(v)
    sum_ref[...] = jnp.broadcast_to(jnp.sum(d * d, keepdims=True), sum_ref.shape)


def moments(slot, grad, mom, before=()):
    _, part, wide = mom.shape
    block = pl.BlockSpec((1, part, wide), lambda n: (slot, 0, 0))
    return pl.pallas_call(
        lambda *refs: moment_kernel(slot, *refs),
        grid=(1,),
        out_shape=(
            jax.ShapeDtypeStruct(mom.shape, f32),
            jax.ShapeDtypeStruct((8, 128), f32),
        ),
        in_specs=[pl.BlockSpec((part, wide), lambda n: (0, 0)), block] + [HB] * len(before),
        out_specs=(block, pl.BlockSpec((8, 128), lambda n: (0, 0))),
        input_output_aliases={2 + i: i for i in range(len(before))},
        compiler_params=params(24),
        cost_estimate=cost(5 * mom.size, 5 * mom.size),
    )(grad, mom, *before)


def lane_block(n):
    return (n + 127) // 128 * 128


def cut_kernel(pos_ref, rows_ref, plus_ref, minus_ref, pad_ref):
    slots, part, wide = rows_ref.shape
    count = wide // part
    gap = pad_ref.shape[1] // count
    pos = pos_ref[0]
    for s in range(slots):
        for k in range(count):
            pad_ref[:, k * gap : k * gap + part] = rows_ref[s, :, k * part : (k + 1) * part]

        def block(step):
            start = pl.multiple_of(lax.rem(pos + step, count) * gap, 128)
            return pad_ref[:, pl.ds(start, gap)][:, :part]

        diag = block(0)
        for j, value in enumerate((block(3), diag, block(2))):
            at = (3 * s + j) * part
            plus_ref[:, at : at + part] = value
        mine = slice(s * part, (s + 1) * part)
        minus_ref[:part, mine] = diag
        minus_ref[part:, mine] = block(1)


def cut(pos, rows):
    slots, part, wide = rows.shape
    return pl.pallas_call(
        cut_kernel,
        out_shape=(
            jax.ShapeDtypeStruct((part, 3 * slots * part), bf16),
            jax.ShapeDtypeStruct((2 * part, slots * part), bf16),
        ),
        in_specs=[SM, VM],
        out_specs=(VM, VM),
        scratch_shapes=[pltpu.VMEM((part, wide // part * lane_block(part)), bf16)],
        compiler_params=params(WHOLE),
        cost_estimate=cost(0, 8 * rows.size),
        name="cut",
    )(pos, rows)


def patch_kernel(shards, s, pos_ref, rows_ref, plus_ref, minus_ref, far_ref, out_hbm, out_ref, sem):
    part, wide = rows_ref.shape[1:]
    count = wide // part
    gap = out_ref.shape[1] // count
    each = wide // shards
    pos = pos_ref[0]
    row = lax.broadcasted_iota(jnp.int32, (part, gap), 0)
    col = lax.broadcasted_iota(jnp.int32, (part, gap), 1)
    place = (col == (row // each) * lifted(each) + lax.rem(row, each)).astype(f32).astype(bf16)

    def put(a, b, value, flip):
        rows = pl.ds(pl.multiple_of(a * part, 16), part)
        at = pl.ds(pl.multiple_of(b * gap, 128), gap)
        out_ref[rows, at] = dot(value, place, TN if flip else NN).astype(bf16)

    def at(step):
        return lax.rem(pos + step, count)

    for k in range(count):
        own = rows_ref[0, :, k * part : (k + 1) * part]
        put(pos, k, own, False)
        put(k, pos, own, True)
    edge = plus_ref[:, 3 * s * part : (3 * s + 1) * part]
    put(at(3), at(2), edge, False)
    put(at(2), at(3), edge, True)
    put(at(3), at(3), plus_ref[:, (3 * s + 1) * part : (3 * s + 2) * part], False)
    edge = plus_ref[:, (3 * s + 2) * part : (3 * s + 3) * part]
    put(at(3), at(1), edge, False)
    put(at(1), at(3), edge, True)
    mine = slice(s * part, (s + 1) * part)
    put(at(1), at(1), minus_ref[:part, mine], False)
    put(at(1), at(2), minus_ref[part:, mine], False)
    put(at(2), at(1), minus_ref[part:, mine], True)
    put(at(2), at(2), far_ref[:, mine], False)
    copy = pltpu.make_async_copy(out_ref, out_hbm, sem)
    copy.start()
    copy.wait()


def lifted(n):
    return (n + 7) // 8 * 8


def patch(slot, pos, shards, rows, plus, minus, far):
    _, part, wide = rows.shape
    count = wide // part
    gap = lane_block(shards // count * lifted(wide // shards))
    shape = (wide, count * gap)

    def whole(x):
        return pl.BlockSpec(x.shape, lambda n: (0, 0))

    return pl.pallas_call(
        lambda *refs: patch_kernel(shards, slot, *refs),
        grid=(1,),
        out_shape=jax.ShapeDtypeStruct(shape, bf16),
        in_specs=[
            SM,
            pl.BlockSpec((1, part, wide), lambda n: (slot, 0, 0)),
            whole(plus),
            whole(minus),
            whole(far),
        ],
        out_specs=HB,
        scratch_shapes=[pltpu.VMEM(shape, bf16), pltpu.SemaphoreType.DMA],
        compiler_params=params(24),
        cost_estimate=cost(wide * wide * part, 3 * wide * wide),
    )(pos, rows, plus, minus, far)


def spread(pos, count, parts, full_ref, sems):
    part = parts[0].shape[0]
    copies = []
    for i, (piece, step) in enumerate(zip(parts, (0, count - 1, 1, 2))):
        start = pl.multiple_of(lax.rem(pos + step, count) * part, 16)
        copies.append(
            pltpu.make_async_copy(piece, full_ref.at[pl.ds(start, part), :], sems.at[i])
        )
    return copies


def pieces_of(value):
    high = value.astype(bf16).astype(f32)
    rest = jnp.where(high < 3e38, value - high, 0.0)
    mid = rest.astype(bf16).astype(f32)
    return high, mid, rest - mid


def precond_kernel(count, shards, slot, *refs):
    pos_ref, right_ref, adam_ref, root_ref = refs[:4]
    grads = refs[4:8]
    out_hbm = refs[8]
    full_ref, root_buf, right_buf, prod_ref, pre_ref, out_ref, sems = refs[9:]
    first = spread(pos_ref[0], count, grads, full_ref, sems)
    first.append(pltpu.make_async_copy(right_ref.at[slot], right_buf, sems.at[4]))
    second = pltpu.make_async_copy(root_ref, root_buf, sems.at[5])
    for c in first:
        c.start()
    second.start()
    part, wide = right_buf.shape
    gap = root_buf.shape[1] // count
    for c in first:
        c.wait()
    step = wide // 3
    for n in range(3):
        cols = slice(n * step, (n + 1) * step)
        prod_ref[:, cols] = dot(right_buf[...], full_ref[:, cols], NN).astype(bf16)
    second.wait()
    total = jnp.zeros((1, 1), f32)
    for k in range(count):
        got = dot(prod_ref[...], root_buf[:, k * gap : (k + 1) * gap], NN)
        pre_ref[k] = got
        total = total + jnp.sum(got * got, keepdims=True)
    lane = lax.broadcasted_iota(jnp.int32, (8, 128), 1)
    extra = jnp.zeros((8, 128), f32)
    for i, value in enumerate(pieces_of(total) + pieces_of(adam_ref[0:1, 0:1])):
        extra = jnp.where(lane == 32 + i, value, extra)
    lift = lifted(wide // shards)
    blank = jnp.zeros((lane_block(part) - part, gap), f32)
    for k in range(count):
        turned = jnp.concatenate([pre_ref[k], blank], axis=0).T
        for j in range(shards // count):
            block = pack(turned[j * lift : (j + 1) * lift], extra)
            out_ref[k * (shards // count) + j] = block.astype(bf16)
    last = pltpu.make_async_copy(out_ref, out_hbm, sems.at[0])
    last.start()
    last.wait()


def precondition(pos, count, shards, slot, right, adam, root, grads):
    part, wide = grads[0].shape
    long = root.shape[1]
    gap = long // count
    return pl.pallas_call(
        lambda *refs: precond_kernel(count, shards, slot, *refs),
        out_shape=jax.ShapeDtypeStruct((shards, PACKED, 128), bf16),
        in_specs=[SM, HB, VM, HB] + [HB] * 4,
        out_specs=HB,
        scratch_shapes=[
            pltpu.VMEM((wide, wide), bf16),
            pltpu.VMEM((wide, long), bf16),
            pltpu.VMEM((part, wide), bf16),
            pltpu.VMEM((part, wide), bf16),
            pltpu.VMEM((count, part, gap), f32),
            pltpu.VMEM((shards, PACKED, 128), bf16),
            pltpu.SemaphoreType.DMA((6,)),
        ],
        compiler_params=params(WHOLE),
        cost_estimate=cost(4 * part * wide * wide, 4 * wide * wide),
    )(pos, right, adam, root, *grads)


def gram_kernel(count, slot, *refs):
    pos_ref, left_ref, right_ref = refs[:3]
    grads = refs[3:7]
    outl_ref, outr_ref, full_ref, own_ref, sems = refs[7 + 2 * slot :]
    n = pl.program_id(0)
    pos = pos_ref[0]
    wide = full_ref.shape[1]
    part = own_ref.shape[1]
    step = outl_ref.shape[2]

    @pl.when(n == 0)
    def _():
        copies = spread(pos, count, grads, full_ref, sems)
        for c in copies:
            c.start()
        for c in copies:
            c.wait()
        for k in range(count):

            @pl.when(pos == k)
            def _():
                own_ref[...] = full_ref[:, k * part : (k + 1) * part]

    cols = pl.ds(pl.multiple_of(n * step, 128), step)
    left = dot(own_ref[...], full_ref[:, cols], TN)
    outl_ref[0] = stat_decay * left_ref[0] + left / wide
    mine = full_ref[pl.ds(pl.multiple_of(pos * part, 16), part), :]
    right = dot(mine, full_ref[cols, :], NT)
    outr_ref[0] = stat_decay * right_ref[0] + right / wide


def grams(pos, count, slot, left, right, grads, before=()):
    _, part, wide = left.shape
    step = wide // 3
    block = pl.BlockSpec((1, part, step), lambda n: (slot, 0, n))
    shape = jax.ShapeDtypeStruct(left.shape, f32)
    return pl.pallas_call(
        lambda *refs: gram_kernel(count, slot, *refs),
        grid=(3,),
        out_shape=(shape, shape),
        in_specs=[SM, block, block] + [HB] * (4 + len(before)),
        out_specs=(block, block),
        scratch_shapes=[
            pltpu.VMEM((wide, wide), bf16),
            pltpu.VMEM((wide, part), bf16),
            pltpu.SemaphoreType.DMA((4,)),
        ],
        input_output_aliases={7 + i: i for i in range(len(before))},
        compiler_params=params(WHOLE),
        cost_estimate=cost(4 * part * wide * wide, 20 * part * wide),
    )(pos, left, right, *grads, *before)


def sums_kernel(back0_ref, back1_ref, out_ref):
    shards, _, lanes = back0_ref.shape
    lane = lax.broadcasted_iota(jnp.int32, (shards, lanes), 1)
    kept = jnp.zeros((shards, lanes), f32)
    for slot, back in enumerate((back0_ref, back1_ref)):
        first = back[...].astype(f32)[:, 0, :]
        for i in range(2):
            terms = [first[:, 32 + 3 * i + j : 33 + 3 * i + j] for j in range(3)]
            kept = jnp.where(lane == 2 * slot + i, terms[0] + terms[1] + terms[2], kept)
    out_ref[...] = jnp.concatenate([kept.T[:8], jnp.zeros((8, lanes - shards), f32)], axis=1)


def partial_sums(back0, back1):
    shards = back0.shape[0]
    block = pl.BlockSpec((shards, 8, 128), lambda n: (0, PACKED // 8 - 1, 0))
    return pl.pallas_call(
        sums_kernel,
        grid=(1,),
        out_shape=jax.ShapeDtypeStruct((8, 128), f32),
        in_specs=[block, block],
        out_specs=pl.BlockSpec((8, 128), lambda n: (0, 0)),
        compiler_params=params(8),
        name="sums",
    )(back0, back1)


def place_kernel(owner_ref, back0_ref, back1_ref, out_ref, where_ref, table_ref, wide_ref):
    fill_slots(owner_ref, table_ref)
    rows, _, _ = out_ref.shape
    lane = lax.broadcasted_iota(jnp.int32, (1, where_ref.shape[2]), 1)
    where_ref[...] = jnp.zeros(where_ref.shape, f32)

    @pl.loop(0, back0_ref.shape[0])
    def _(d):
        for rank, back_ref in enumerate((back0_ref, back1_ref)):
            b = table_ref[2 * d + rank]

            @pl.when(b >= 0)
            def _():

                def put(row, column, value):
                    height, width = value.shape
                    wide_ref[b, row : row + height, column : column + width] = value

                unpack(back_ref[d].astype(f32), put)
                where_ref[rank, pl.ds(b, 1), :] = (lane == d).astype(f32)

    out_ref[...] = pltpu.einshape("brc->rbc", wide_ref[...])[:rows]


def place(owner_list, backs, rows, part):
    nb = owner_list.shape[0]
    shards = backs[0].shape[0]
    return pl.pallas_call(
        place_kernel,
        out_shape=(
            jax.ShapeDtypeStruct((rows, nb, part), f32),
            jax.ShapeDtypeStruct((2, nb, 128), f32),
        ),
        in_specs=[SM, VM, VM],
        out_specs=(VM, VM),
        scratch_shapes=[
            pltpu.SMEM((2 * shards,), jnp.int32),
            pltpu.VMEM((nb, lifted(rows), part), f32),
        ],
        compiler_params=params(8),
        cost_estimate=cost(0, 8 * rows * nb * part),
        name="place",
    )(owner_list, *backs)


def final_kernel(entries, s0_ref, s1_ref, where_ref, dir_ref, w_ref, out_ref):
    total = (s0_ref[...] + s1_ref[...]) / entries

    def factor(rank):
        pre_mean, adam_mean = total[2 * rank : 2 * rank + 1], total[2 * rank + 1 : 2 * rank + 2]
        return -learn_rate * (jnp.sqrt(adam_mean) / jnp.sqrt(pre_mean + graft_eps))

    chosen = where_ref[0] * factor(0) + where_ref[1] * factor(1)
    scale = jnp.sum(chosen, axis=1, keepdims=True)
    for r in range(out_ref.shape[0]):
        out_ref[r] = w_ref[r] + scale * dir_ref[r]


def final(sums, where, direction, weights, entries):
    return pl.pallas_call(
        lambda *refs: final_kernel(entries, *refs),
        out_shape=jax.ShapeDtypeStruct(weights.shape, f32),
        in_specs=[VM] * 5,
        out_specs=VM,
        compiler_params=params(8),
        name="final",
    )(*sums, where, direction, weights)


def step(gradients, weights, owner_list, left_stats, right_stats, left_root, right_root, moment):
    shards = lax.axis_size("shard")
    count = lax.axis_size("tensor")
    pos = lax.axis_index("tensor").astype(jnp.int32).reshape(1)

    def shift(x, by):
        ring = [(i, (i + by) % count) for i in range(count)]
        return lax.ppermute(x, "tensor", ring)

    def exchange(x):
        return lax.all_to_all(x, "shard", 0, 0, tiled=True)

    left_rows = jnp.swapaxes(left_root, 1, 2)
    right_rows = jnp.swapaxes(right_root, 1, 2)
    grad_rows = jnp.swapaxes(gradients, 0, 1)
    mom_rows = jnp.swapaxes(moment, 1, 2)
    part, wide = left_rows.shape[1:]

    plus, minus = cut(pos, left_rows)
    plus, minus = shift(plus, 1), shift(minus, -1)
    far = shift(minus[:part], -1)

    parts, grads = [], []
    for s in range(2):
        send = pick(s, owner_list, grad_rows, shards)
        own = turn(exchange(send), gradients.shape[1], part)
        l, r = shift(own, 1), shift(own, -1)
        far_part = shift(l, 1) if s == 0 else shift(r, -1)
        parts.append(own)
        grads.append((own, l, r, far_part))
    before, roots, adams, backs = (), [], [], []
    for s in range(2):
        new_moment, adam = moments(s, parts[s], mom_rows, before)
        before = (new_moment,)
        adams.append(adam)
        roots.append(patch(s, pos, shards, left_rows, plus, minus, far))
    for s in range(2):
        update = precondition(pos, count, shards, s, right_rows, adams[s], roots[s], grads[s])
        backs.append(exchange(update))
    stats = ()
    for s in range(2):
        stats = grams(pos, count, s, left_stats, right_stats, grads[s], stats)
    new_left, new_right = stats
    mine = partial_sums(backs[0], backs[1])

    def swap(x, flip):
        pairs = [(i, i ^ flip) for i in range(count)]
        return lax.ppermute(x, "tensor", pairs)

    mine = mine + swap(mine, 1)
    sums = [mine, swap(mine, 3)]
    rows = weights.shape[1]
    direction, where = place(owner_list, backs, rows, part)
    w_rows = jnp.swapaxes(weights, 0, 1)
    new_weights = final(sums, where, direction, w_rows, float(wide * wide))
    return (
        jnp.swapaxes(new_weights, 0, 1),
        new_left,
        new_right,
        jnp.swapaxes(new_moment, 1, 2),
    )


def solution(mesh):
    return jax.shard_map(
        step,
        mesh=mesh,
        in_specs=(
            P(None, "shard", "tensor"),
            P(None, "shard", "tensor"),
            P(),
            P("shard", "tensor", None),
            P("shard", "tensor", None),
            P("shard", None, "tensor"),
            P("shard", None, "tensor"),
            P("shard", None, "tensor"),
        ),
        out_specs=(
            P(None, "shard", "tensor"),
            P("shard", "tensor", None),
            P("shard", "tensor", None),
            P("shard", None, "tensor"),
        ),
        check_vma=False,
    )
```

```python
import jax
import jax.numpy as jnp
from jax import lax
from jax.experimental import pallas as pl
from jax.experimental.pallas import tpu as pltpu
from jax.sharding import PartitionSpec as P


stat_decay = 0.95
moment_decay = 0.95
learn_rate = 0.02
graft_eps = 1e-06

f32 = jnp.float32
bf16 = jnp.bfloat16
VM = pl.BlockSpec(memory_space=pltpu.VMEM)
SM = pl.BlockSpec(memory_space=pltpu.SMEM)
HB = pl.BlockSpec(memory_space=pltpu.HBM)

NN = (((1,), (0,)), ((), ()))
NT = (((1,), (1,)), ((), ()))
TN = (((0,), (0,)), ((), ()))


def dot(a, b, dims):
    return lax.dot_general(a, b, dims, preferred_element_type=f32)


WHOLE = 63


def params(mib, **kw):
    return pltpu.CompilerParams(vmem_limit_bytes=mib * 1024 * 1024, **kw)


def cost(flops, nbytes):
    return pl.CostEstimate(flops=int(flops), bytes_accessed=int(nbytes), transcendentals=0)


def fill_slots(owner_ref, table_ref):
    @pl.loop(0, table_ref.shape[0])
    def _(i):
        table_ref[i] = -1

    @pl.loop(0, owner_ref.shape[0])
    def _(b):
        first = 2 * owner_ref[b]
        rank = (table_ref[first] >= 0).astype(jnp.int32)
        table_ref[first + rank] = b


PACKED = 88


def pack(x, extra=None):
    row = lax.broadcasted_iota(jnp.int32, (8, 128), 0)
    lane = lax.broadcasted_iota(jnp.int32, (8, 128), 1)
    tail = x[:, 256:384]
    wrapped = tail[0:8]
    for j in range(1, 4):
        turned = pltpu.roll(tail[8 * j : 8 * j + 8], 32 * j, 1)
        wrapped = jnp.where(lane >= 32 * j, turned, wrapped)
    low = jnp.where(row < 4, x[32:40, 0:128], pltpu.roll(x[32:40, 128:256], 4, 0))
    last = tail[32:40] if extra is None else jnp.where(lane < 32, tail[32:40], extra)
    return jnp.concatenate([x[0:32, 0:128], x[0:32, 128:256], wrapped, low, last], axis=0)


def unpack(y, put):
    put(0, 0, y[0:32])
    put(0, 128, y[32:64])
    for j in range(4):
        part = y[64:72] if j == 0 else pltpu.roll(y[64:72], 128 - 32 * j, 1)
        put(8 * j, 256, part[:, :32])
    put(32, 0, y[72:76])
    put(32, 128, pltpu.roll(y[72:80], 4, 0)[0:4])
    put(32, 256, y[80:84, :32])


def pick_kernel(rank, owner_ref, grad_hbm, out_hbm, table_ref, grad_ref, wide_ref, out_ref, sems):
    rows, _, width = grad_ref.shape
    spans = (slice(0, 16), slice(16, rows))
    loads = [
        pltpu.make_async_copy(grad_hbm.at[x], grad_ref.at[x], sems.at[4 + i])
        for i, x in enumerate(spans)
    ]
    for c in loads:
        c.start()
    fill_slots(owner_ref, table_ref)
    for c, x in zip(loads, spans):
        c.wait()
        wide_ref[:, x, :width] = pltpu.einshape("rbc->brc", grad_ref[x].astype(f32))

    per = out_ref.shape[0] // 4

    def sent(i):
        rows = pl.ds(i * per, per)
        return pltpu.make_async_copy(out_ref.at[rows], out_hbm.at[rows], sems.at[i])

    for i in range(4):

        @pl.loop(i * per, (i + 1) * per)
        def _(d):
            b = table_ref[2 * d + rank]

            @pl.when(b >= 0)
            def _():
                out_ref[d] = pack(wide_ref[b]).astype(bf16)

            @pl.when(b < 0)
            def _():
                out_ref[d] = jnp.zeros(out_ref.shape[1:], bf16)

        sent(i).start()
    for i in range(4):
        sent(i).wait()


def pick(rank, owner_list, gradients, shards):
    rows, nb, width = gradients.shape
    return pl.pallas_call(
        lambda *refs: pick_kernel(rank, *refs),
        out_shape=jax.ShapeDtypeStruct((shards, PACKED, 128), bf16),
        in_specs=[SM, HB],
        out_specs=HB,
        scratch_shapes=[
            pltpu.SMEM((2 * shards,), jnp.int32),
            pltpu.VMEM((rows, nb, width), bf16),
            pltpu.VMEM((nb, 40, 384), f32),
            pltpu.VMEM((shards, PACKED, 128), bf16),
            pltpu.SemaphoreType.DMA((6,)),
        ],
        compiler_params=params(WHOLE),
        cost_estimate=cost(0, 5 * gradients.size),
    )(owner_list, gradients)


def turn_kernel(got_ref, out_hbm, wide_ref, out_ref, sem):
    count = got_ref.shape[0]
    rows = wide_ref.shape[0] // count
    for s in range(count):

        def put(row, column, value):
            at = s * rows + row
            wide_ref[at : at + value.shape[0], column : column + value.shape[1]] = value

        unpack(got_ref[s].astype(f32), put)
    out_ref[...] = wide_ref[...].T.astype(bf16)
    pltpu.make_async_copy(out_ref, out_hbm, sem).start()
    pltpu.make_async_copy(out_ref, out_hbm, sem).wait()


def turn(got, rows, width):
    count = got.shape[0]
    return pl.pallas_call(
        turn_kernel,
        out_shape=jax.ShapeDtypeStruct((width, count * rows), bf16),
        in_specs=[VM],
        out_specs=HB,
        scratch_shapes=[
            pltpu.VMEM((count * rows, width), f32),
            pltpu.VMEM((width, count * rows), bf16),
            pltpu.SemaphoreType.DMA,
        ],
        compiler_params=params(8),
        cost_estimate=cost(0, 5 * got.size),
        name="turn",
    )(got)


def moment_kernel(slot, grad_ref, mom_ref, *refs):
    out_ref, sum_ref = refs[slot:]
    g = grad_ref[...].astype(f32)
    v = moment_decay * mom_ref[0] + ((1.0 - moment_decay) * g) * g
    out_ref[0] = v
    d = g * lax.rsqrt(v)
    sum_ref[...] = jnp.broadcast_to(jnp.sum(d * d, keepdims=True), sum_ref.shape)


def moments(slot, grad, mom, before=()):
    _, part, wide = mom.shape
    block = pl.BlockSpec((1, part, wide), lambda n: (slot, 0, 0))
    return pl.pallas_call(
        lambda *refs: moment_kernel(slot, *refs),
        grid=(1,),
        out_shape=(
            jax.ShapeDtypeStruct(mom.shape, f32),
            jax.ShapeDtypeStruct((8, 128), f32),
        ),
        in_specs=[pl.BlockSpec((part, wide), lambda n: (0, 0)), block] + [HB] * len(before),
        out_specs=(block, pl.BlockSpec((8, 128), lambda n: (0, 0))),
        input_output_aliases={2 + i: i for i in range(len(before))},
        compiler_params=params(24),
        cost_estimate=cost(5 * mom.size, 5 * mom.size),
    )(grad, mom, *before)


def lane_block(n):
    return (n + 127) // 128 * 128


def position():
    return lax.axis_index("tensor").astype(jnp.int32)


def cut_kernel(rows_ref, plus_ref, minus_ref, pad_ref):
    slots, _, wide = rows_ref.shape
    part = minus_ref.shape[2] // slots
    count = wide // part
    gap = pad_ref.shape[1] // count
    pos = position()
    for s in range(slots):
        for k in range(count):
            pad_ref[:, k * gap : k * gap + part] = rows_ref[s, :, k * part : (k + 1) * part]

        def block(step):
            start = pl.multiple_of(lax.rem(pos + step, count) * gap, 128)
            return pad_ref[:, pl.ds(start, gap)][:, :part]

        diag = block(0)
        for j, value in enumerate((block(3), diag, block(2))):
            at = (3 * s + j) * part
            plus_ref[:, at : at + part] = value
        mine = slice(s * part, (s + 1) * part)
        minus_ref[0, :, mine] = diag
        minus_ref[1, :, mine] = block(1)


def cut(rows):
    slots, part, wide = rows.shape
    chunk = part
    plus, minus = pl.pallas_call(
        cut_kernel,
        grid=(part // chunk,),
        out_shape=(
            jax.ShapeDtypeStruct((part, 3 * slots * part), bf16),
            jax.ShapeDtypeStruct((2, part, slots * part), bf16),
        ),
        in_specs=[pl.BlockSpec((slots, chunk, wide), lambda i: (0, i, 0))],
        out_specs=(
            pl.BlockSpec((chunk, 3 * slots * part), lambda i: (i, 0)),
            pl.BlockSpec((2, chunk, slots * part), lambda i: (0, i, 0)),
        ),
        scratch_shapes=[pltpu.VMEM((chunk, wide // part * lane_block(part)), bf16)],
        compiler_params=params(WHOLE),
        cost_estimate=cost(0, 8 * rows.size),
        name="cut",
    )(rows)
    return plus, minus.reshape(2 * part, slots * part)


def patch_kernel(shards, s, rows_ref, plus_ref, minus_ref, far_ref, out_hbm, out_ref, sem):
    part, wide = rows_ref.shape[1:]
    count = wide // part
    gap = out_ref.shape[1] // count
    each = wide // shards
    pos = position()
    row = lax.broadcasted_iota(jnp.int32, (part, gap), 0)
    col = lax.broadcasted_iota(jnp.int32, (part, gap), 1)
    place = (col == (row // each) * lifted(each) + lax.rem(row, each)).astype(f32).astype(bf16)

    def put(a, b, value, flip):
        rows = pl.ds(pl.multiple_of(a * part, 16), part)
        at = pl.ds(pl.multiple_of(b * gap, 128), gap)
        out_ref[rows, at] = dot(value, place, TN if flip else NN).astype(bf16)

    def at(step):
        return lax.rem(pos + step, count)

    for k in range(count):
        own = rows_ref[0, :, k * part : (k + 1) * part]
        put(pos, k, own, False)
        put(k, pos, own, True)
    edge = plus_ref[:, 3 * s * part : (3 * s + 1) * part]
    put(at(3), at(2), edge, False)
    put(at(2), at(3), edge, True)
    put(at(3), at(3), plus_ref[:, (3 * s + 1) * part : (3 * s + 2) * part], False)
    edge = plus_ref[:, (3 * s + 2) * part : (3 * s + 3) * part]
    put(at(3), at(1), edge, False)
    put(at(1), at(3), edge, True)
    mine = slice(s * part, (s + 1) * part)
    put(at(1), at(1), minus_ref[:part, mine], False)
    put(at(1), at(2), minus_ref[part:, mine], False)
    put(at(2), at(1), minus_ref[part:, mine], True)
    put(at(2), at(2), far_ref[:, mine], False)
    copy = pltpu.make_async_copy(out_ref, out_hbm, sem)
    copy.start()
    copy.wait()


def lifted(n):
    return (n + 7) // 8 * 8


def patch(slot, shards, rows, plus, minus, far):
    _, part, wide = rows.shape
    count = wide // part
    gap = lane_block(shards // count * lifted(wide // shards))
    shape = (wide, count * gap)

    def whole(x):
        return pl.BlockSpec(x.shape, lambda n: (0, 0))

    return pl.pallas_call(
        lambda *refs: patch_kernel(shards, slot, *refs),
        grid=(1,),
        out_shape=jax.ShapeDtypeStruct(shape, bf16),
        in_specs=[
            pl.BlockSpec((1, part, wide), lambda n: (slot, 0, 0)),
            whole(plus),
            whole(minus),
            whole(far),
        ],
        out_specs=HB,
        scratch_shapes=[pltpu.VMEM(shape, bf16), pltpu.SemaphoreType.DMA],
        compiler_params=params(24),
        cost_estimate=cost(wide * wide * part, 3 * wide * wide),
    )(rows, plus, minus, far)


def spread(pos, count, parts, full_ref, sems):
    part = parts[0].shape[0]
    copies = []
    for i, (piece, step) in enumerate(zip(parts, (0, count - 1, 1, 2))):
        start = pl.multiple_of(lax.rem(pos + step, count) * part, 16)
        copies.append(
            pltpu.make_async_copy(piece, full_ref.at[pl.ds(start, part), :], sems.at[i])
        )
    return copies


def pieces_of(value):
    high = value.astype(bf16).astype(f32)
    rest = jnp.where(high < 3e38, value - high, 0.0)
    mid = rest.astype(bf16).astype(f32)
    return high, mid, rest - mid


def precond_kernel(count, shards, slot, *refs):
    right_ref, adam_ref, root_ref = refs[:3]
    grads = refs[3:7]
    out_hbm = refs[7]
    full_ref, root_buf, right_buf, adam_buf, prod_ref, pre_ref, out_ref, sems = refs[8:]
    part, wide = right_buf.shape
    gap = root_buf.shape[1] // count
    step = wide // 3
    first = pltpu.make_async_copy(right_ref.at[slot], right_buf, sems.at[3, 0])
    second = pltpu.make_async_copy(root_ref, root_buf, sems.at[3, 1])
    third = pltpu.make_async_copy(adam_ref, adam_buf, sems.at[3, 2])
    chunks = [
        spread(
            position(),
            count,
            [g.at[:, pl.ds(n * step, step)] for g in grads],
            full_ref.at[:, pl.ds(n * step, step)],
            sems.at[n],
        )
        for n in range(3)
    ]
    first.start()
    for c in sum(chunks, []):
        c.start()
    second.start()
    third.start()
    first.wait()
    for n in range(3):
        cols = slice(n * step, (n + 1) * step)
        for c in chunks[n]:
            c.wait()
        prod_ref[:, cols] = dot(right_buf[...], full_ref[:, cols], NN).astype(bf16)
    second.wait()
    third.wait()
    total = jnp.zeros((1, 1), f32)
    for k in range(count):
        got = dot(prod_ref[...], root_buf[:, k * gap : (k + 1) * gap], NN)
        pre_ref[k] = got
        total = total + jnp.sum(got * got, keepdims=True)
    lane = lax.broadcasted_iota(jnp.int32, (8, 128), 1)
    extra = jnp.zeros((8, 128), f32)
    for i, value in enumerate(pieces_of(total) + pieces_of(adam_buf[0:1, 0:1])):
        extra = jnp.where(lane == 32 + i, value, extra)
    lift = lifted(wide // shards)
    blank = jnp.zeros((lane_block(part) - part, gap), f32)
    per = shards // count
    sent = [
        pltpu.make_async_copy(
            out_ref.at[pl.ds(k * per, per)], out_hbm.at[pl.ds(k * per, per)], sems.at[4, k]
        )
        for k in range(count)
    ]
    for k in range(count):
        turned = jnp.concatenate([pre_ref[k], blank], axis=0).T
        for j in range(shards // count):
            block = pack(turned[j * lift : (j + 1) * lift], extra)
            out_ref[k * (shards // count) + j] = block.astype(bf16)
        sent[k].start()
    for c in sent:
        c.wait()


def precondition(count, shards, slot, right, adam, root, grads):
    part, wide = grads[0].shape
    long = root.shape[1]
    gap = long // count
    return pl.pallas_call(
        lambda *refs: precond_kernel(count, shards, slot, *refs),
        out_shape=jax.ShapeDtypeStruct((shards, PACKED, 128), bf16),
        in_specs=[HB] * 7,
        out_specs=HB,
        scratch_shapes=[
            pltpu.VMEM((wide, wide), bf16),
            pltpu.VMEM((wide, long), bf16),
            pltpu.VMEM((part, wide), bf16),
            pltpu.VMEM((8, 128), f32),
            pltpu.VMEM((part, wide), bf16),
            pltpu.VMEM((count, part, gap), f32),
            pltpu.VMEM((shards, PACKED, 128), bf16),
            pltpu.SemaphoreType.DMA((5, count)),
        ],
        compiler_params=params(WHOLE),
        cost_estimate=cost(4 * part * wide * wide, 4 * wide * wide),
    )(right, adam, root, *grads)


def gram_kernel(count, slot, *refs):
    left_ref, right_ref = refs[:2]
    grads = refs[2:6]
    outl_ref, outr_ref, full_ref, own_ref, sems = refs[6 + 2 * slot :]
    n = pl.program_id(0)
    pos = position()
    wide = full_ref.shape[1]
    part = own_ref.shape[1]
    step = outl_ref.shape[2]

    @pl.when(n == 0)
    def _():
        copies = spread(pos, count, grads, full_ref, sems)
        for c in copies:
            c.start()
        for c in copies:
            c.wait()
        for k in range(count):

            @pl.when(pos == k)
            def _():
                own_ref[...] = full_ref[:, k * part : (k + 1) * part]

    cols = pl.ds(pl.multiple_of(n * step, 128), step)
    left = dot(own_ref[...], full_ref[:, cols], TN)
    outl_ref[0] = stat_decay * left_ref[0] + left / wide
    mine = full_ref[pl.ds(pl.multiple_of(pos * part, 16), part), :]
    right = dot(mine, full_ref[cols, :], NT)
    outr_ref[0] = stat_decay * right_ref[0] + right / wide


def grams(count, slot, left, right, grads, before=()):
    _, part, wide = left.shape
    step = wide // 3
    block = pl.BlockSpec((1, part, step), lambda n: (slot, 0, n))
    shape = jax.ShapeDtypeStruct(left.shape, f32)
    return pl.pallas_call(
        lambda *refs: gram_kernel(count, slot, *refs),
        grid=(3,),
        out_shape=(shape, shape),
        in_specs=[block, block] + [HB] * (4 + len(before)),
        out_specs=(block, block),
        scratch_shapes=[
            pltpu.VMEM((wide, wide), bf16),
            pltpu.VMEM((wide, part), bf16),
            pltpu.SemaphoreType.DMA((4,)),
        ],
        input_output_aliases={6 + i: i for i in range(len(before))},
        compiler_params=params(WHOLE),
        cost_estimate=cost(4 * part * wide * wide, 20 * part * wide),
    )(left, right, *grads, *before)


def sums_kernel(back0_ref, back1_ref, out_ref):
    shards, _, lanes = back0_ref.shape
    lane = lax.broadcasted_iota(jnp.int32, (shards, lanes), 1)
    kept = jnp.zeros((shards, lanes), f32)
    for slot, back in enumerate((back0_ref, back1_ref)):
        first = back[...].astype(f32)[:, 0, :]
        for i in range(2):
            terms = [first[:, 32 + 3 * i + j : 33 + 3 * i + j] for j in range(3)]
            kept = jnp.where(lane == 2 * slot + i, terms[0] + terms[1] + terms[2], kept)
    out_ref[...] = jnp.concatenate([kept.T[:8], jnp.zeros((8, lanes - shards), f32)], axis=1)


def partial_sums(back0, back1):
    shards = back0.shape[0]
    block = pl.BlockSpec((shards, 8, 128), lambda n: (0, PACKED // 8 - 1, 0))
    return pl.pallas_call(
        sums_kernel,
        grid=(1,),
        out_shape=jax.ShapeDtypeStruct((8, 128), f32),
        in_specs=[block, block],
        out_specs=pl.BlockSpec((8, 128), lambda n: (0, 0)),
        compiler_params=params(8),
        name="sums",
    )(back0, back1)


def place_kernel(owner_ref, back0_ref, back1_ref, out_ref, where_ref, table_ref, wide_ref):
    fill_slots(owner_ref, table_ref)
    rows, _, _ = out_ref.shape
    lane = lax.broadcasted_iota(jnp.int32, (1, where_ref.shape[2]), 1)
    where_ref[...] = jnp.zeros(where_ref.shape, f32)

    @pl.loop(0, back0_ref.shape[0])
    def _(d):
        for rank, back_ref in enumerate((back0_ref, back1_ref)):
            b = table_ref[2 * d + rank]

            @pl.when(b >= 0)
            def _():

                def put(row, column, value):
                    height, width = value.shape
                    wide_ref[b, row : row + height, column : column + width] = value

                unpack(back_ref[d].astype(f32), put)
                where_ref[rank, pl.ds(b, 1), :] = (lane == d).astype(f32)

    out_ref[...] = pltpu.einshape("brc->rbc", wide_ref[...])[:rows]


def place(owner_list, backs, rows, part):
    nb = owner_list.shape[0]
    shards = backs[0].shape[0]
    return pl.pallas_call(
        place_kernel,
        out_shape=(
            jax.ShapeDtypeStruct((rows, nb, part), f32),
            jax.ShapeDtypeStruct((2, nb, 128), f32),
        ),
        in_specs=[SM, VM, VM],
        out_specs=(VM, VM),
        scratch_shapes=[
            pltpu.SMEM((2 * shards,), jnp.int32),
            pltpu.VMEM((nb, lifted(rows), part), f32),
        ],
        compiler_params=params(8),
        cost_estimate=cost(0, 8 * rows * nb * part),
        name="place",
    )(owner_list, *backs)


def final_kernel(entries, s0_ref, s1_ref, where_ref, dir_ref, w_ref, out_ref):
    total = (s0_ref[...] + s1_ref[...]) / entries

    def factor(rank):
        pre_mean, adam_mean = total[2 * rank : 2 * rank + 1], total[2 * rank + 1 : 2 * rank + 2]
        return -learn_rate * (jnp.sqrt(adam_mean) / jnp.sqrt(pre_mean + graft_eps))

    chosen = where_ref[0] * factor(0) + where_ref[1] * factor(1)
    scale = jnp.sum(chosen, axis=1, keepdims=True)
    for r in range(out_ref.shape[0]):
        out_ref[r] = w_ref[r] + scale * dir_ref[r]


def final(sums, where, direction, weights, entries):
    return pl.pallas_call(
        lambda *refs: final_kernel(entries, *refs),
        out_shape=jax.ShapeDtypeStruct(weights.shape, f32),
        in_specs=[VM] * 5,
        out_specs=VM,
        compiler_params=params(8),
        name="final",
    )(*sums, where, direction, weights)


def step(gradients, weights, owner_list, left_stats, right_stats, left_root, right_root, moment):
    shards = lax.axis_size("shard")
    count = lax.axis_size("tensor")

    def shift(x, by):
        ring = [(i, (i + by) % count) for i in range(count)]
        return lax.ppermute(x, "tensor", ring)

    def exchange(x):
        return lax.all_to_all(x, "shard", 0, 0, tiled=True)

    left_rows = jnp.swapaxes(left_root, 1, 2)
    right_rows = jnp.swapaxes(right_root, 1, 2)
    grad_rows = jnp.swapaxes(gradients, 0, 1)
    mom_rows = jnp.swapaxes(moment, 1, 2)
    part, wide = left_rows.shape[1:]

    plus, minus = cut(left_rows)
    plus, minus = shift(plus, 1), shift(minus, -1)
    far = shift(minus[:part], -1)

    parts, grads = [], []
    for s in range(2):
        send = pick(s, owner_list, grad_rows, shards)
        own = turn(exchange(send), gradients.shape[1], part)
        l, r = shift(own, 1), shift(own, -1)
        far_part = shift(l, 1) if s == 0 else shift(r, -1)
        parts.append(own)
        grads.append((own, l, r, far_part))
    before, roots, adams, backs = (), [], [], []
    for s in range(2):
        new_moment, adam = moments(s, parts[s], mom_rows, before)
        before = (new_moment,)
        adams.append(adam)
        roots.append(patch(s, shards, left_rows, plus, minus, far))
    for s in range(2):
        update = precondition(count, shards, s, right_rows, adams[s], roots[s], grads[s])
        backs.append(exchange(update))
    stats = ()
    for s in range(2):
        stats = grams(count, s, left_stats, right_stats, grads[s], stats)
    new_left, new_right = stats
    mine = partial_sums(backs[0], backs[1])

    def swap(x, flip):
        pairs = [(i, i ^ flip) for i in range(count)]
        return lax.ppermute(x, "tensor", pairs)

    mine = mine + swap(mine, 1)
    sums = [mine, swap(mine, 3)]
    rows = weights.shape[1]
    direction, where = place(owner_list, backs, rows, part)
    w_rows = jnp.swapaxes(weights, 0, 1)
    new_weights = final(sums, where, direction, w_rows, float(wide * wide))
    return (
        jnp.swapaxes(new_weights, 0, 1),
        new_left,
        new_right,
        jnp.swapaxes(new_moment, 1, 2),
    )


def solution(mesh):
    return jax.shard_map(
        step,
        mesh=mesh,
        in_specs=(
            P(None, "shard", "tensor"),
            P(None, "shard", "tensor"),
            P(),
            P("shard", "tensor", None),
            P("shard", "tensor", None),
            P("shard", None, "tensor"),
            P("shard", None, "tensor"),
            P("shard", None, "tensor"),
        ),
        out_specs=(
            P(None, "shard", "tensor"),
            P("shard", "tensor", None),
            P("shard", "tensor", None),
            P("shard", None, "tensor"),
        ),
        check_vma=False,
    )
```

```python
import jax
import jax.numpy as jnp
from jax import lax
from jax.experimental import pallas as pl
from jax.experimental.pallas import tpu as pltpu
from jax.sharding import PartitionSpec as P


stat_decay = 0.95
moment_decay = 0.95
learn_rate = 0.02
graft_eps = 1e-06

f32 = jnp.float32
bf16 = jnp.bfloat16
VM = pl.BlockSpec(memory_space=pltpu.VMEM)
SM = pl.BlockSpec(memory_space=pltpu.SMEM)
HB = pl.BlockSpec(memory_space=pltpu.HBM)

NN = (((1,), (0,)), ((), ()))
NT = (((1,), (1,)), ((), ()))
TN = (((0,), (0,)), ((), ()))


def dot(a, b, dims):
    return lax.dot_general(a, b, dims, preferred_element_type=f32)


WHOLE = 63


def params(mib, **kw):
    return pltpu.CompilerParams(vmem_limit_bytes=mib * 1024 * 1024, **kw)


def cost(flops, nbytes):
    return pl.CostEstimate(flops=int(flops), bytes_accessed=int(nbytes), transcendentals=0)


def fill_slots(owner_ref, table_ref):
    @pl.loop(0, table_ref.shape[0])
    def _(i):
        table_ref[i] = -1

    @pl.loop(0, owner_ref.shape[0])
    def _(b):
        first = 2 * owner_ref[b]
        rank = (table_ref[first] >= 0).astype(jnp.int32)
        table_ref[first + rank] = b


PACKED = 88


def pack(x, extra=None):
    row = lax.broadcasted_iota(jnp.int32, (8, 128), 0)
    lane = lax.broadcasted_iota(jnp.int32, (8, 128), 1)
    tail = x[:, 256:384]
    wrapped = tail[0:8]
    for j in range(1, 4):
        turned = pltpu.roll(tail[8 * j : 8 * j + 8], 32 * j, 1)
        wrapped = jnp.where(lane >= 32 * j, turned, wrapped)
    low = jnp.where(row < 4, x[32:40, 0:128], pltpu.roll(x[32:40, 128:256], 4, 0))
    last = tail[32:40] if extra is None else jnp.where(lane < 32, tail[32:40], extra)
    return jnp.concatenate([x[0:32, 0:128], x[0:32, 128:256], wrapped, low, last], axis=0)


def unpack(y, put):
    put(0, 0, y[0:32])
    put(0, 128, y[32:64])
    for j in range(4):
        part = y[64:72] if j == 0 else pltpu.roll(y[64:72], 128 - 32 * j, 1)
        put(8 * j, 256, part[:, :32])
    put(32, 0, y[72:76])
    put(32, 128, pltpu.roll(y[72:80], 4, 0)[0:4])
    put(32, 256, y[80:84, :32])


def pick_kernel(rank, owner_ref, grad_hbm, out_hbm, table_ref, grad_ref, wide_ref, out_ref, sems):
    rows, _, width = grad_ref.shape
    spans = (slice(0, 16), slice(16, rows))
    loads = [
        pltpu.make_async_copy(grad_hbm.at[x], grad_ref.at[x], sems.at[4 + i])
        for i, x in enumerate(spans)
    ]
    for c in loads:
        c.start()
    fill_slots(owner_ref, table_ref)
    for c, x in zip(loads, spans):
        c.wait()
        wide_ref[:, x, :width] = pltpu.einshape("rbc->brc", grad_ref[x].astype(f32))

    per = out_ref.shape[0] // 4

    def sent(i):
        rows = pl.ds(i * per, per)
        return pltpu.make_async_copy(out_ref.at[rows], out_hbm.at[rows], sems.at[i])

    for i in range(4):

        @pl.loop(i * per, (i + 1) * per)
        def _(d):
            b = table_ref[2 * d + rank]

            @pl.when(b >= 0)
            def _():
                out_ref[d] = pack(wide_ref[b]).astype(bf16)

            @pl.when(b < 0)
            def _():
                out_ref[d] = jnp.zeros(out_ref.shape[1:], bf16)

        sent(i).start()
    for i in range(4):
        sent(i).wait()


def pick(rank, owner_list, gradients, shards):
    rows, nb, width = gradients.shape
    return pl.pallas_call(
        lambda *refs: pick_kernel(rank, *refs),
        out_shape=jax.ShapeDtypeStruct((shards, PACKED, 128), bf16),
        in_specs=[SM, HB],
        out_specs=HB,
        scratch_shapes=[
            pltpu.SMEM((2 * shards,), jnp.int32),
            pltpu.VMEM((rows, nb, width), bf16),
            pltpu.VMEM((nb, 40, 384), f32),
            pltpu.VMEM((shards, PACKED, 128), bf16),
            pltpu.SemaphoreType.DMA((6,)),
        ],
        compiler_params=params(WHOLE),
        cost_estimate=cost(0, 5 * gradients.size),
    )(owner_list, gradients)


def turn_kernel(got_ref, out_ref, wide_ref):
    count = got_ref.shape[0]
    rows = wide_ref.shape[0] // count
    for s in range(count):

        def put(row, column, value):
            at = s * rows + row
            wide_ref[at : at + value.shape[0], column : column + value.shape[1]] = value

        unpack(got_ref[s].astype(f32), put)
    out_ref[...] = wide_ref[...].T.astype(bf16)


def turn(got, rows, width):
    count = got.shape[0]
    return pl.pallas_call(
        turn_kernel,
        out_shape=jax.ShapeDtypeStruct((width, count * rows), bf16),
        in_specs=[VM],
        out_specs=VM,
        scratch_shapes=[pltpu.VMEM((count * rows, width), f32)],
        compiler_params=params(8),
        cost_estimate=cost(0, 5 * got.size),
        name="turn",
    )(got)


def moment_kernel(slot, grad_ref, mom_ref, *refs):
    out_ref, sum_ref = refs[slot:]
    g = grad_ref[...].astype(f32)
    v = moment_decay * mom_ref[0] + ((1.0 - moment_decay) * g) * g
    out_ref[0] = v
    d = g * lax.rsqrt(v)
    sum_ref[...] = jnp.broadcast_to(jnp.sum(d * d, keepdims=True), sum_ref.shape)


def moments(slot, grad, mom, before=()):
    _, part, wide = mom.shape
    block = pl.BlockSpec((1, part, wide), lambda n: (slot, 0, 0))
    return pl.pallas_call(
        lambda *refs: moment_kernel(slot, *refs),
        grid=(1,),
        out_shape=(
            jax.ShapeDtypeStruct(mom.shape, f32),
            jax.ShapeDtypeStruct((8, 128), f32),
        ),
        in_specs=[pl.BlockSpec((part, wide), lambda n: (0, 0)), block] + [HB] * len(before),
        out_specs=(block, pl.BlockSpec((8, 128), lambda n: (0, 0))),
        input_output_aliases={2 + i: i for i in range(len(before))},
        compiler_params=params(24),
        cost_estimate=cost(5 * mom.size, 5 * mom.size),
    )(grad, mom, *before)


def lane_block(n):
    return (n + 127) // 128 * 128


def position():
    return lax.axis_index("tensor").astype(jnp.int32)


def cut_kernel(rows_ref, plus_ref, minus_ref, pad_ref):
    slots, _, wide = rows_ref.shape
    part = minus_ref.shape[2] // slots
    count = wide // part
    gap = pad_ref.shape[1] // count
    pos = position()
    for s in range(slots):
        for k in range(count):
            pad_ref[:, k * gap : k * gap + part] = rows_ref[s, :, k * part : (k + 1) * part]

        def block(step):
            start = pl.multiple_of(lax.rem(pos + step, count) * gap, 128)
            return pad_ref[:, pl.ds(start, gap)][:, :part]

        diag = block(0)
        for j, value in enumerate((block(3), diag, block(2))):
            at = (3 * s + j) * part
            plus_ref[:, at : at + part] = value
        mine = slice(s * part, (s + 1) * part)
        minus_ref[0, :, mine] = diag
        minus_ref[1, :, mine] = block(1)


def cut(rows):
    slots, part, wide = rows.shape
    chunk = part
    plus, minus = pl.pallas_call(
        cut_kernel,
        grid=(part // chunk,),
        out_shape=(
            jax.ShapeDtypeStruct((part, 3 * slots * part), bf16),
            jax.ShapeDtypeStruct((2, part, slots * part), bf16),
        ),
        in_specs=[pl.BlockSpec((slots, chunk, wide), lambda i: (0, i, 0))],
        out_specs=(
            pl.BlockSpec((chunk, 3 * slots * part), lambda i: (i, 0)),
            pl.BlockSpec((2, chunk, slots * part), lambda i: (0, i, 0)),
        ),
        scratch_shapes=[pltpu.VMEM((chunk, wide // part * lane_block(part)), bf16)],
        compiler_params=params(WHOLE),
        cost_estimate=cost(0, 8 * rows.size),
        name="cut",
    )(rows)
    return plus, minus.reshape(2 * part, slots * part)


def patch_kernel(shards, s, rows_ref, plus_ref, minus_ref, far_ref, out_hbm, out_ref, sem):
    part, wide = rows_ref.shape[1:]
    count = wide // part
    gap = out_ref.shape[1] // count
    each = wide // shards
    pos = position()
    row = lax.broadcasted_iota(jnp.int32, (part, gap), 0)
    col = lax.broadcasted_iota(jnp.int32, (part, gap), 1)
    place = (col == (row // each) * lifted(each) + lax.rem(row, each)).astype(f32).astype(bf16)

    def put(a, b, value, flip):
        rows = pl.ds(pl.multiple_of(a * part, 16), part)
        at = pl.ds(pl.multiple_of(b * gap, 128), gap)
        out_ref[rows, at] = dot(value, place, TN if flip else NN).astype(bf16)

    def at(step):
        return lax.rem(pos + step, count)

    for k in range(count):
        own = rows_ref[0, :, k * part : (k + 1) * part]
        put(pos, k, own, False)
        put(k, pos, own, True)
    edge = plus_ref[:, 3 * s * part : (3 * s + 1) * part]
    put(at(3), at(2), edge, False)
    put(at(2), at(3), edge, True)
    put(at(3), at(3), plus_ref[:, (3 * s + 1) * part : (3 * s + 2) * part], False)
    edge = plus_ref[:, (3 * s + 2) * part : (3 * s + 3) * part]
    put(at(3), at(1), edge, False)
    put(at(1), at(3), edge, True)
    mine = slice(s * part, (s + 1) * part)
    put(at(1), at(1), minus_ref[:part, mine], False)
    put(at(1), at(2), minus_ref[part:, mine], False)
    put(at(2), at(1), minus_ref[part:, mine], True)
    put(at(2), at(2), far_ref[:, mine], False)
    copy = pltpu.make_async_copy(out_ref, out_hbm, sem)
    copy.start()
    copy.wait()


def lifted(n):
    return (n + 7) // 8 * 8


def patch(slot, shards, rows, plus, minus, far):
    _, part, wide = rows.shape
    count = wide // part
    gap = lane_block(shards // count * lifted(wide // shards))
    shape = (wide, count * gap)

    def whole(x):
        return pl.BlockSpec(x.shape, lambda n: (0, 0))

    return pl.pallas_call(
        lambda *refs: patch_kernel(shards, slot, *refs),
        grid=(1,),
        out_shape=jax.ShapeDtypeStruct(shape, bf16),
        in_specs=[
            pl.BlockSpec((1, part, wide), lambda n: (slot, 0, 0)),
            whole(plus),
            whole(minus),
            whole(far),
        ],
        out_specs=HB,
        scratch_shapes=[pltpu.VMEM(shape, bf16), pltpu.SemaphoreType.DMA],
        compiler_params=params(WHOLE),
        cost_estimate=cost(wide * wide * part, 3 * wide * wide),
    )(rows, plus, minus, far)


def spread(pos, count, parts, full_ref, sems):
    part = parts[0].shape[0]
    copies = []
    for i, (piece, step) in enumerate(zip(parts, (0, count - 1, 1, 2))):
        start = pl.multiple_of(lax.rem(pos + step, count) * part, 16)
        copies.append(
            pltpu.make_async_copy(piece, full_ref.at[pl.ds(start, part), :], sems.at[i])
        )
    return copies


def pieces_of(value):
    high = value.astype(bf16).astype(f32)
    rest = jnp.where(high < 3e38, value - high, 0.0)
    mid = rest.astype(bf16).astype(f32)
    return high, mid, rest - mid


def precond_kernel(count, shards, slot, *refs):
    right_ref, adam_ref, root_ref = refs[:3]
    grads = refs[3:7]
    out_hbm = refs[7]
    full_ref, root_buf, right_buf, adam_buf, prod_ref, pre_ref, out_ref, sems = refs[8:]
    part, wide = right_buf.shape
    gap = root_buf.shape[1] // count
    step = wide // 3
    first = pltpu.make_async_copy(right_ref.at[slot], right_buf, sems.at[3, 0])
    second = pltpu.make_async_copy(root_ref, root_buf, sems.at[3, 1])
    third = pltpu.make_async_copy(adam_ref, adam_buf, sems.at[3, 2])
    chunks = [
        spread(
            position(),
            count,
            [g.at[:, pl.ds(n * step, step)] for g in grads],
            full_ref.at[:, pl.ds(n * step, step)],
            sems.at[n],
        )
        for n in range(3)
    ]
    first.start()
    for c in sum(chunks, []):
        c.start()
    second.start()
    third.start()
    first.wait()
    for n in range(3):
        cols = slice(n * step, (n + 1) * step)
        for c in chunks[n]:
            c.wait()
        prod_ref[:, cols] = dot(right_buf[...], full_ref[:, cols], NN).astype(bf16)
    second.wait()
    third.wait()
    total = jnp.zeros((1, 1), f32)
    for k in range(count):
        got = dot(prod_ref[...], root_buf[:, k * gap : (k + 1) * gap], NN)
        pre_ref[k] = got
        total = total + jnp.sum(got * got, keepdims=True)
    lane = lax.broadcasted_iota(jnp.int32, (8, 128), 1)
    extra = jnp.zeros((8, 128), f32)
    for i, value in enumerate(pieces_of(total) + pieces_of(adam_buf[0:1, 0:1])):
        extra = jnp.where(lane == 32 + i, value, extra)
    lift = lifted(wide // shards)
    blank = jnp.zeros((lane_block(part) - part, gap), f32)
    per = shards // count
    sent = [
        pltpu.make_async_copy(
            out_ref.at[pl.ds(k * per, per)], out_hbm.at[pl.ds(k * per, per)], sems.at[4, k]
        )
        for k in range(count)
    ]
    for k in range(count):
        turned = jnp.concatenate([pre_ref[k], blank], axis=0).T
        for j in range(shards // count):
            block = pack(turned[j * lift : (j + 1) * lift], extra)
            out_ref[k * (shards // count) + j] = block.astype(bf16)
        sent[k].start()
    for c in sent:
        c.wait()


def precondition(count, shards, slot, right, adam, root, grads):
    part, wide = grads[0].shape
    long = root.shape[1]
    gap = long // count
    return pl.pallas_call(
        lambda *refs: precond_kernel(count, shards, slot, *refs),
        out_shape=jax.ShapeDtypeStruct((shards, PACKED, 128), bf16),
        in_specs=[HB] * 7,
        out_specs=HB,
        scratch_shapes=[
            pltpu.VMEM((wide, wide), bf16),
            pltpu.VMEM((wide, long), bf16),
            pltpu.VMEM((part, wide), bf16),
            pltpu.VMEM((8, 128), f32),
            pltpu.VMEM((part, wide), bf16),
            pltpu.VMEM((count, part, gap), f32),
            pltpu.VMEM((shards, PACKED, 128), bf16),
            pltpu.SemaphoreType.DMA((5, count)),
        ],
        compiler_params=params(WHOLE),
        cost_estimate=cost(4 * part * wide * wide, 4 * wide * wide),
    )(right, adam, root, *grads)


def gram_kernel(count, slot, *refs):
    left_ref, right_ref = refs[:2]
    grads = refs[2:6]
    outl_ref, outr_ref, full_ref, own_ref, sems = refs[6 + 2 * slot :]
    n = pl.program_id(0)
    pos = position()
    wide = full_ref.shape[1]
    part = own_ref.shape[1]
    step = outl_ref.shape[2]

    @pl.when(n == 0)
    def _():
        copies = spread(pos, count, grads, full_ref, sems)
        for c in copies:
            c.start()
        for c in copies:
            c.wait()
        for k in range(count):

            @pl.when(pos == k)
            def _():
                own_ref[...] = full_ref[:, k * part : (k + 1) * part]

    cols = pl.ds(pl.multiple_of(n * step, 128), step)
    left = dot(own_ref[...], full_ref[:, cols], TN)
    outl_ref[0] = stat_decay * left_ref[0] + left / wide
    mine = full_ref[pl.ds(pl.multiple_of(pos * part, 16), part), :]
    right = dot(mine, full_ref[cols, :], NT)
    outr_ref[0] = stat_decay * right_ref[0] + right / wide


def grams(count, slot, left, right, grads, before=()):
    _, part, wide = left.shape
    step = wide // 3
    block = pl.BlockSpec((1, part, step), lambda n: (slot, 0, n))
    shape = jax.ShapeDtypeStruct(left.shape, f32)
    return pl.pallas_call(
        lambda *refs: gram_kernel(count, slot, *refs),
        grid=(3,),
        out_shape=(shape, shape),
        in_specs=[block, block] + [HB] * (4 + len(before)),
        out_specs=(block, block),
        scratch_shapes=[
            pltpu.VMEM((wide, wide), bf16),
            pltpu.VMEM((wide, part), bf16),
            pltpu.SemaphoreType.DMA((4,)),
        ],
        input_output_aliases={6 + i: i for i in range(len(before))},
        compiler_params=params(WHOLE),
        cost_estimate=cost(4 * part * wide * wide, 20 * part * wide),
    )(left, right, *grads, *before)


def sums_kernel(back0_ref, back1_ref, out_ref):
    shards, _, lanes = back0_ref.shape
    lane = lax.broadcasted_iota(jnp.int32, (shards, lanes), 1)
    kept = jnp.zeros((shards, lanes), f32)
    for slot, back in enumerate((back0_ref, back1_ref)):
        first = back[...].astype(f32)[:, 0, :]
        for i in range(2):
            terms = [first[:, 32 + 3 * i + j : 33 + 3 * i + j] for j in range(3)]
            kept = jnp.where(lane == 2 * slot + i, terms[0] + terms[1] + terms[2], kept)
    out_ref[...] = jnp.concatenate([kept.T[:8], jnp.zeros((8, lanes - shards), f32)], axis=1)


def partial_sums(back0, back1):
    shards = back0.shape[0]
    block = pl.BlockSpec((shards, 8, 128), lambda n: (0, PACKED // 8 - 1, 0))
    return pl.pallas_call(
        sums_kernel,
        grid=(1,),
        out_shape=jax.ShapeDtypeStruct((8, 128), f32),
        in_specs=[block, block],
        out_specs=pl.BlockSpec((8, 128), lambda n: (0, 0)),
        compiler_params=params(8),
        name="sums",
    )(back0, back1)


def place_kernel(owner_ref, back0_ref, back1_ref, out_ref, where_ref, table_ref, wide_ref):
    fill_slots(owner_ref, table_ref)
    rows, _, _ = out_ref.shape
    lane = lax.broadcasted_iota(jnp.int32, (1, where_ref.shape[2]), 1)
    where_ref[...] = jnp.zeros(where_ref.shape, f32)

    @pl.loop(0, back0_ref.shape[0])
    def _(d):
        for rank, back_ref in enumerate((back0_ref, back1_ref)):
            b = table_ref[2 * d + rank]

            @pl.when(b >= 0)
            def _():

                def put(row, column, value):
                    height, width = value.shape
                    wide_ref[b, row : row + height, column : column + width] = value

                unpack(back_ref[d].astype(f32), put)
                where_ref[rank, pl.ds(b, 1), :] = (lane == d).astype(f32)

    out_ref[...] = pltpu.einshape("brc->rbc", wide_ref[...])[:rows]


def place(owner_list, backs, rows, part):
    nb = owner_list.shape[0]
    shards = backs[0].shape[0]
    return pl.pallas_call(
        place_kernel,
        out_shape=(
            jax.ShapeDtypeStruct((rows, nb, part), f32),
            jax.ShapeDtypeStruct((2, nb, 128), f32),
        ),
        in_specs=[SM, VM, VM],
        out_specs=(VM, VM),
        scratch_shapes=[
            pltpu.SMEM((2 * shards,), jnp.int32),
            pltpu.VMEM((nb, lifted(rows), part), f32),
        ],
        compiler_params=params(8),
        cost_estimate=cost(0, 8 * rows * nb * part),
        name="place",
    )(owner_list, *backs)


def final_kernel(entries, s0_ref, s1_ref, where_ref, dir_ref, w_ref, out_ref):
    total = (s0_ref[...] + s1_ref[...]) / entries

    def factor(rank):
        pre_mean, adam_mean = total[2 * rank : 2 * rank + 1], total[2 * rank + 1 : 2 * rank + 2]
        return -learn_rate * (jnp.sqrt(adam_mean) / jnp.sqrt(pre_mean + graft_eps))

    chosen = where_ref[0] * factor(0) + where_ref[1] * factor(1)
    scale = jnp.sum(chosen, axis=1, keepdims=True)
    for r in range(out_ref.shape[0]):
        out_ref[r] = w_ref[r] + scale * dir_ref[r]


def final(sums, where, direction, weights, entries):
    return pl.pallas_call(
        lambda *refs: final_kernel(entries, *refs),
        out_shape=jax.ShapeDtypeStruct(weights.shape, f32),
        in_specs=[VM] * 5,
        out_specs=VM,
        compiler_params=params(8),
        name="final",
    )(*sums, where, direction, weights)


def step(gradients, weights, owner_list, left_stats, right_stats, left_root, right_root, moment):
    shards = lax.axis_size("shard")
    count = lax.axis_size("tensor")

    def shift(x, by):
        ring = [(i, (i + by) % count) for i in range(count)]
        return lax.ppermute(x, "tensor", ring)

    def exchange(x):
        return lax.all_to_all(x, "shard", 0, 0, tiled=True)

    left_rows = jnp.swapaxes(left_root, 1, 2)
    right_rows = jnp.swapaxes(right_root, 1, 2)
    grad_rows = jnp.swapaxes(gradients, 0, 1)
    mom_rows = jnp.swapaxes(moment, 1, 2)
    part, wide = left_rows.shape[1:]

    plus, minus = cut(left_rows)
    plus, minus = shift(plus, 1), shift(minus, -1)
    far = shift(minus[:part], -1)

    parts, grads = [], []
    for s in range(2):
        send = pick(s, owner_list, grad_rows, shards)
        own = turn(exchange(send), gradients.shape[1], part)
        l, r = shift(own, 1), shift(own, -1)
        far_part = shift(l, 1) if s == 0 else shift(r, -1)
        parts.append(own)
        grads.append((own, l, r, far_part))
    before, roots, adams, backs = (), [], [], []
    for s in range(2):
        new_moment, adam = moments(s, parts[s], mom_rows, before)
        before = (new_moment,)
        adams.append(adam)
        roots.append(patch(s, shards, left_rows, plus, minus, far))
    for s in range(2):
        update = precondition(count, shards, s, right_rows, adams[s], roots[s], grads[s])
        backs.append(exchange(update))
    stats = ()
    for s in range(2):
        stats = grams(count, s, left_stats, right_stats, grads[s], stats)
    new_left, new_right = stats
    mine = partial_sums(backs[0], backs[1])

    def swap(x, flip):
        pairs = [(i, i ^ flip) for i in range(count)]
        return lax.ppermute(x, "tensor", pairs)

    mine = mine + swap(mine, 1)
    sums = [mine, swap(mine, 3)]
    rows = weights.shape[1]
    direction, where = place(owner_list, backs, rows, part)
    w_rows = jnp.swapaxes(weights, 0, 1)
    new_weights = final(sums, where, direction, w_rows, float(wide * wide))
    return (
        jnp.swapaxes(new_weights, 0, 1),
        new_left,
        new_right,
        jnp.swapaxes(new_moment, 1, 2),
    )


def solution(mesh):
    return jax.shard_map(
        step,
        mesh=mesh,
        in_specs=(
            P(None, "shard", "tensor"),
            P(None, "shard", "tensor"),
            P(),
            P("shard", "tensor", None),
            P("shard", "tensor", None),
            P("shard", None, "tensor"),
            P("shard", None, "tensor"),
            P("shard", None, "tensor"),
        ),
        out_specs=(
            P(None, "shard", "tensor"),
            P("shard", "tensor", None),
            P("shard", "tensor", None),
            P("shard", None, "tensor"),
        ),
        check_vma=False,
    )
```
